32 devices in a mesh: row: 16 (over z, x, core), col: 2 (over y).
Axes of the slice: x: 2, y: 2, z: 4, core: 2. Of those that a mesh axis runs over, the one named last changes fastest.
Arguments:
- features: bfloat16 [16384, 256], P(('row', 'col')), may hold values from -6 to 6
- grad_out: bfloat16 [16384, 256], P(('row', 'col')), may hold values from -6 to 6
- weight: bfloat16 [256, 256], replicated, may hold values from -0.375 to 0.375
- tiles: bfloat16 [6144, 128, 128], P(('row', 'col')), may hold values from -0.125 to 0.125
- tile_row: int32 [6144], P(('row', 'col')), may hold values from 0 to 7
- tile_col: int32 [6144], P(('row', 'col')), may hold values from 0 to 63
- tile_count: int32 [32], P(('row', 'col')), may hold values from 24 to 192, as said below
Outputs:
- grad_features: bfloat16 [16384, 256], P(('row', 'col'))
- grad_weight: float32 [256, 256], replicated
The draws below stay inside these ranges and needn't reach their ends.
Inputs may be any that keep to these rules, and one draw needn't show every extreme that they name: `tile_count`: exactly 192 on some device in every draw; slots of a device from its count on are not part of the adjacency.
All inputs are finite; a program needn't handle non-finite values.
Results may differ from the reference program's by a relative error of at most 0.02.
Values may be sent and summed in bfloat16 or wider, within the bound.
A program may use at most 128 MiB of HBM per device.

```python
import jax
import jax.numpy as jnp
from jax import lax

F = 256
TILE = 128
MAXT = 192
V = 16384
RT = 8
CT = 64
N_ROW = 16
N_COL = 2
DEVICES = 32


def draw_tile_count(key, part):
    light_load = jax.random.randint(jax.random.fold_in(key, 11), (DEVICES,), MAXT // 8, MAXT // 3 + 1)
    heavy_load = jax.random.randint(jax.random.fold_in(key, 12), (DEVICES,), MAXT // 2, MAXT + 1)
    heavy_pick = jax.random.randint(jax.random.fold_in(key, 13), (DEVICES,), 0, 8) == 0
    counts = jnp.where(heavy_pick, heavy_load, light_load)
    top_device = jax.random.randint(jax.random.fold_in(key, 14), (), 0, DEVICES)
    counts = jnp.where(jnp.arange(DEVICES, dtype=jnp.int32) == top_device, MAXT, counts)
    return counts.astype(jnp.int32)


def with_ends(drawn, stream_key, low, largest):
    spot = [jax.random.randint(jax.random.fold_in(stream_key, axis), (), 0, length) for axis, length in enumerate(drawn.shape)]
    widest = drawn.shape.index(max(drawn.shape))
    beside = spot[:widest] + [(spot[widest] + 1) % drawn.shape[widest]] + spot[widest + 1:]
    return drawn.at[tuple(spot)].set(low).at[tuple(beside)].set(largest)


def steps_of(stream_key, extent, shards, low, largest):
    gain = 1.0
    for axis_at, parts in shards:
        draws = jax.random.uniform(jax.random.fold_in(jax.random.fold_in(stream_key, 6), axis_at), (parts,), jnp.float32, low / len(shards), largest / len(shards))
        gain = gain * jnp.repeat(jnp.exp(draws), extent[axis_at] // parts).reshape((-1,) + (1,) * (len(extent) - 1 - axis_at))
    return gain


def noise(own_key, extent, deviation, bound, cuts=(), kind=jnp.bfloat16):
    result = jax.random.normal(own_key, extent, jnp.float32) * deviation
    if len(cuts) > 0:
        result = steps_of(own_key, extent, cuts, -0.22, 0.18) * result
    return jnp.clip(result, min=-bound, max=bound).astype(kind)


def setup_inputs(seed: int = 0) -> dict:
    arg_keys = jax.random.split(jax.random.key(seed), 8)
    return {
        "features": noise(arg_keys[0], (V, F), 1.0, 6.0, ((0, 32),)),
        "grad_out": noise(arg_keys[1], (V, F), 1.0, 6.0, ((0, 32),)),
        "weight": noise(arg_keys[2], (F, F), F ** -0.5, 0.375),
        "tiles": noise(arg_keys[3], (DEVICES * MAXT, TILE, TILE), (TILE * TILE // 8) ** -0.5, 0.125, ((0, 32),)),
        "tile_row": with_ends(jax.random.randint(arg_keys[4], (DEVICES * MAXT,), 0, RT), jax.random.fold_in(arg_keys[4], 1), 0, RT - 1).astype(jnp.int32),
        "tile_col": with_ends(jax.random.randint(arg_keys[5], (DEVICES * MAXT,), 0, CT), jax.random.fold_in(arg_keys[5], 1), 0, CT - 1).astype(jnp.int32),
        "tile_count": draw_tile_count(jax.random.fold_in(arg_keys[7], 71), 0),
    }


def reference(features, grad_out, weight, tiles, tile_row, tile_col, tile_count):
    devices = N_ROW * N_COL
    tile_size = tiles.shape[1]
    feat_width = weight.shape[0]
    segment = features.shape[0] // devices
    slots = tiles.shape[0] // devices
    row_tiles = N_COL * segment // tile_size
    col_tiles = N_ROW * segment // tile_size
    mixed_rows = jnp.dot(features, weight, preferred_element_type=jnp.float32).astype(jnp.bfloat16)
    panels = mixed_rows.reshape(N_ROW, N_COL, segment, feat_width).transpose(1, 0, 2, 3)
    panels = panels.reshape(N_COL, col_tiles, tile_size, feat_width)
    tile_sets = tiles.reshape(devices, slots, tile_size, tile_size)
    row_ids = tile_row.reshape(devices, slots)
    col_ids = tile_col.reshape(devices, slots)
    live_mask = (jnp.arange(slots, dtype=jnp.int32)[None, :] < tile_count[:, None]).astype(jnp.float32)

    def forward(total, device_index):
        row_index = device_index // N_COL
        col_index = device_index % N_COL
        picked = panels[col_index][col_ids[device_index]]
        product = jnp.einsum("sij,sjf->sif", tile_sets[device_index].astype(jnp.float32),
                             picked.astype(jnp.float32), precision=lax.Precision.HIGHEST)
        product = product * live_mask[device_index][:, None, None]
        return total.at[row_index, row_ids[device_index]].add(product), None

    start = jnp.zeros((N_ROW, row_tiles, tile_size, feat_width), jnp.float32)
    preact = lax.scan(forward, start, jnp.arange(devices, dtype=jnp.int32))[0]
    preact = preact.reshape(devices * segment, feat_width)
    sigmoid_z = jax.nn.sigmoid(preact)
    grad_pre = (grad_out.astype(jnp.float32) * sigmoid_z * (1.0 + preact * (1.0 - sigmoid_z))).astype(jnp.bfloat16)
    grad_blocks = grad_pre.reshape(N_ROW, row_tiles, tile_size, feat_width)

    def backward(total, device_index):
        row_index = device_index // N_COL
        col_index = device_index % N_COL
        picked = grad_blocks[row_index][row_ids[device_index]]
        product = jnp.einsum("sji,sjf->sif", tile_sets[device_index].astype(jnp.float32),
                             picked.astype(jnp.float32), precision=lax.Precision.HIGHEST)
        product = product * live_mask[device_index][:, None, None]
        part = jnp.zeros((col_tiles, tile_size, feat_width), jnp.float32).at[col_ids[device_index]].add(product)
        part = part.astype(jnp.bfloat16).astype(jnp.float32)
        return total.at[col_index].add(part), None

    start_back = jnp.zeros((N_COL, col_tiles, tile_size, feat_width), jnp.float32)
    grad_sum = lax.scan(backward, start_back, jnp.arange(devices, dtype=jnp.int32))[0]
    grad_sum = grad_sum.reshape(N_COL, N_ROW, segment, feat_width).transpose(1, 0, 2, 3)
    grad_panel = grad_sum.reshape(devices * segment, feat_width).astype(jnp.bfloat16)
    grad_features = jnp.dot(grad_panel, weight.T, preferred_element_type=jnp.float32).astype(jnp.bfloat16)
    grad_weight = jnp.dot(features.T, grad_panel, preferred_element_type=jnp.float32)
    return grad_features, grad_weight
```

```python
import functools

import jax
import jax.numpy as jnp
from jax import lax
from jax.experimental import pallas as pl
from jax.experimental.pallas import tpu as pltpu
from jax.sharding import PartitionSpec as P

CHUNK = 16
GROUP = 4


def silu_grad(preact, upstream):
    sigmoid_z = jax.nn.sigmoid(preact)
    return (upstream.astype(jnp.float32) * sigmoid_z * (1.0 + preact * (1.0 - sigmoid_z))).astype(
        jnp.bfloat16
    )


def spread_kernel(transpose, read_ids, write_ids, count_ref, tiles_hbm, panel_ref, out_ref, buf, acc, sems):
    slots, tile_size, _ = tiles_hbm.shape
    out_tiles = out_ref.shape[0] // tile_size
    chunks = slots // CHUNK
    count = count_ref[0]
    live_chunks = (count + CHUNK - 1) // CHUNK

    def fetch(chunk):
        part = pl.ds(chunk * CHUNK, CHUNK)
        return pltpu.make_async_copy(tiles_hbm.at[part], buf.at[part], sems.at[chunk])

    for chunk in range(chunks):

        @pl.when(chunk < live_chunks)
        def _():
            fetch(chunk).start()

    acc[...] = jnp.zeros_like(acc)
    contract = (((0,), (0,)), ((), ())) if transpose else (((1,), (0,)), ((), ()))

    def one(slot, keep):
        src = pl.multiple_of(read_ids[slot] * tile_size, tile_size)
        product = lax.dot_general(
            buf[slot], panel_ref[pl.ds(src, tile_size), :], contract, preferred_element_type=jnp.float32
        )
        return jnp.where(keep, product, 0.0) if keep is not None else product

    def add(slot, product):
        dst = pl.multiple_of(write_ids[slot] * tile_size, tile_size)
        acc[pl.ds(dst, tile_size), :] += product

    def chunk_step(chunk, carry):
        fetch(chunk).wait()
        base = chunk * CHUNK
        groups = jnp.minimum(count - base, CHUNK) // GROUP

        def group_step(group, carry):
            first = base + group * GROUP
            products = [one(first + k, None) for k in range(GROUP)]
            for k in range(GROUP):
                add(first + k, products[k])
            return carry

        lax.fori_loop(0, groups, group_step, 0)

        def tail_step(slot, carry):
            add(slot, one(slot, None))
            return carry

        lax.fori_loop(base + groups * GROUP, jnp.minimum(count, base + CHUNK), tail_step, 0)
        return carry

    lax.fori_loop(0, live_chunks, chunk_step, 0)

    def finish(tile, carry):
        part = pl.ds(pl.multiple_of(tile * tile_size, tile_size), tile_size)
        out_ref[part, :] = acc[part, :].astype(out_ref.dtype)
        return carry

    lax.fori_loop(0, out_tiles, finish, 0)


def spread_tiles(tiles, read_ids, write_ids, count, panel, out_rows, transpose):
    slots, tile_size, _ = tiles.shape
    feat_width = panel.shape[-1]
    return pl.pallas_call(
        functools.partial(spread_kernel, transpose),
        out_shape=jax.ShapeDtypeStruct((out_rows, feat_width), jnp.bfloat16),
        in_specs=[
            pl.BlockSpec(memory_space=pltpu.SMEM),
            pl.BlockSpec(memory_space=pltpu.SMEM),
            pl.BlockSpec(memory_space=pltpu.SMEM),
            pl.BlockSpec(memory_space=pl.ANY),
            pl.BlockSpec(memory_space=pltpu.VMEM),
        ],
        out_specs=pl.BlockSpec(memory_space=pltpu.VMEM),
        scratch_shapes=[
            pltpu.VMEM(tiles.shape, tiles.dtype),
            pltpu.VMEM((out_rows, feat_width), jnp.float32),
            pltpu.SemaphoreType.DMA((slots // CHUNK,)),
        ],
        compiler_params=pltpu.CompilerParams(vmem_limit_bytes=60 * 1024 * 1024),
        name="back" if transpose else "forth",
    )(read_ids, write_ids, count, tiles, panel)


def body(features, grad_out, weight, tiles, tile_row, tile_col, tile_count):
    segment = features.shape[0]
    mixed_rows = jnp.dot(features, weight, preferred_element_type=jnp.float32).astype(jnp.bfloat16)
    panel = lax.all_gather(mixed_rows, "row", axis=0, tiled=True)
    row_span = segment * lax.axis_size("col")
    partial_value = spread_tiles(tiles, tile_col, tile_row, tile_count, panel, row_span, False)
    owned = lax.psum_scatter(partial_value, "col", scatter_dimension=0, tiled=True).astype(jnp.float32)
    grad_block = lax.all_gather(silu_grad(owned, grad_out), "col", axis=0, tiled=True)
    back_terms = spread_tiles(tiles, tile_row, tile_col, tile_count, grad_block, panel.shape[0], True)
    summed = lax.psum_scatter(back_terms, "row", scatter_dimension=0, tiled=True).astype(jnp.float32)
    grad_panel = summed.astype(jnp.bfloat16)
    grad_features = lax.dot_general(
        grad_panel, weight, (((1,), (1,)), ((), ())), preferred_element_type=jnp.float32
    ).astype(jnp.bfloat16)
    local_weight = lax.dot_general(
        features, grad_panel, (((0,), (0,)), ((), ())), preferred_element_type=jnp.float32
    )
    grad_weight = lax.psum(local_weight, ("row", "col"))
    return (grad_features, grad_weight)


def solution(mesh):
    in_specs = (
        P(("row", "col"), None),
        P(("row", "col"), None),
        P(),
        P(("row", "col"), None, None),
        P(("row", "col")),
        P(("row", "col")),
        P(("row", "col")),
    )
    out_specs = (P(("row", "col"), None), P())
    return jax.shard_map(body, mesh=mesh, in_specs=in_specs, out_specs=out_specs, check_vma=False)
```

```python
import functools

import jax
import jax.numpy as jnp
from jax import lax
from jax.experimental import pallas as pl
from jax.experimental.pallas import tpu as pltpu
from jax.sharding import PartitionSpec as P

CHUNK = 16
GROUP = 4


MESH = pl.DeviceIdType.MESH
VMEM_SPEC = pl.BlockSpec(memory_space=pltpu.VMEM)
LIMIT = 60 * 1024 * 1024


def silu_grad(preact, upstream):
    sigmoid_z = jax.nn.sigmoid(preact)
    return (upstream.astype(jnp.float32) * sigmoid_z * (1.0 + preact * (1.0 - sigmoid_z))).astype(
        jnp.bfloat16
    )


def ring_place(chip, chips):
    half = lax.div(chip, 2)
    return jnp.where(lax.rem(chip, 2) == 0, half, chips - 1 - half)


def ring_chip(place, chips):
    place = lax.rem(place + 2 * chips, chips)
    return jnp.where(place < chips // 2, 2 * place, 2 * (chips - 1 - place) + 1)


def row_device(chip, core):
    return {"row": chip * 2 + core}


def greet(partners):
    barrier = pltpu.get_barrier_semaphore()
    for partner in partners:
        pl.semaphore_signal(barrier, inc=1, device_id=partner, device_id_type=MESH)
    pl.semaphore_wait(barrier, len(partners))


def remote(src, dst, send_sem, recv_sem, device):
    return pltpu.make_async_remote_copy(
        src_ref=src, dst_ref=dst, send_sem=send_sem, recv_sem=recv_sem, device_id=device, device_id_type=MESH
    )


def gather_kernel(n_row, f_ref, w_ref, fp_ref, mp_ref, ssem, rsem, xs, xr, os, orr):
    chips = n_row // 2
    seg = f_ref.shape[0]
    half = seg // 2
    me = lax.axis_index("row")
    core = lax.rem(me, 2)
    chip = lax.div(me, 2)
    place = ring_place(chip, chips)
    ways = (1, -1)
    nexts = [row_device(ring_chip(place + way, chips), core) for way in ways]
    sibling = row_device(chip, 1 - core)
    greet(nexts + [sibling])
    far = chips // 2
    plans = [
        [(h, k) for k in range(1, far) for h in (way, 1 - way)] + [(way, far)] for way in (0, 1)
    ]
    count = len(plans[0])

    def rows_of(owner, h):
        return pl.ds(pl.multiple_of(owner * seg + h * half, half), half)

    def origin(way, k):
        return ring_chip(place - ways[way] * k, chips)

    def hop(way, i):
        h, k = plans[way][i]
        if k == 1:
            src = f_ref.at[pl.ds(h * half, half)]
            rows = rows_of(me, h)
        else:
            rows = rows_of(origin(way, k - 1) * 2 + core, h)
            src = fp_ref.at[rows]
        return remote(src, fp_ref.at[rows], ssem.at[way, i], rsem.at[way, i], nexts[way])

    def across(way, i):
        h, k = plans[way][i]
        rows = rows_of(origin(way, k) * 2 + core, h)
        return remote(fp_ref.at[rows], fp_ref.at[rows], xs.at[way, i], xr.at[way, i], sibling)

    def own_across(h):
        return remote(
            f_ref.at[pl.ds(h * half, half)], fp_ref.at[rows_of(me, h)], os.at[h], orr.at[h], sibling
        )

    def mix(owner, h):
        rows = rows_of(owner, h)
        mp_ref[rows, :] = jnp.dot(
            fp_ref[rows, :], w_ref[...], preferred_element_type=jnp.float32
        ).astype(mp_ref.dtype)

    for i in (0, 1):
        for way in (0, 1):
            hop(way, i).start()
    for h in (0, 1):
        own_across(h).start()
    fp_ref[pl.ds(pl.multiple_of(me * seg, seg), seg), :] = f_ref[...]
    for h in (0, 1):
        mix(me, h)
    for i in range(count):
        for way in (0, 1):
            hop(way, i).wait_recv()
            if i + 2 < count:
                hop(way, i + 2).start()
            across(way, i).start()
        if i == 0:
            for h in (0, 1):
                own_across(h).wait_recv()
                mix(chip * 2 + 1 - core, h)
        for way in (0, 1):
            h, k = plans[way][i]
            mix(origin(way, k) * 2 + core, h)
            if i > 0:
                h, k = plans[way][i - 1]
                across(way, i - 1).wait_recv()
                mix(origin(way, k) * 2 + 1 - core, h)
    for way in (0, 1):
        h, k = plans[way][count - 1]
        across(way, count - 1).wait_recv()
        mix(origin(way, k) * 2 + 1 - core, h)
    for way in (0, 1):
        for i in range(count):
            hop(way, i).wait_send()
            across(way, i).wait_send()
    for h in (0, 1):
        own_across(h).wait_send()


def gather_mixed(features, weight, n_row):
    seg, feat_width = features.shape
    count = n_row // 2 - 1
    shape = jax.ShapeDtypeStruct((n_row * seg, feat_width), features.dtype)
    dma = pltpu.SemaphoreType.DMA
    return pl.pallas_call(
        functools.partial(gather_kernel, n_row),
        out_shape=(shape, shape),
        in_specs=[VMEM_SPEC] * 2,
        out_specs=(VMEM_SPEC, VMEM_SPEC),
        scratch_shapes=[dma((2, count))] * 4 + [dma((2,))] * 2,
        compiler_params=pltpu.CompilerParams(
            collective_id=0, has_side_effects=True, vmem_limit_bytes=LIMIT
        ),
        name="gather",
    )(features, weight)


PARTS = 4


def exchange_kernel(n_col, part_ref, up_ref, out_ref, inbox, ssem, rsem, gs, gr):
    seg = up_ref.shape[0]
    step = seg // PARTS
    me = lax.axis_index("col")
    others = [lax.rem(me + o, n_col) for o in range(1, n_col)]
    greet([{"col": other} for other in others])

    def rows_of(owner, c):
        return pl.ds(pl.multiple_of(owner * seg + c * step, step), step)

    def there(o, c):
        return remote(
            part_ref.at[rows_of(others[o], c)],
            inbox.at[o, pl.ds(c * step, step)],
            ssem.at[o, c],
            rsem.at[o, c],
            {"col": others[o]},
        )

    def back(o, c):
        rows = rows_of(me, c)
        return remote(out_ref.at[rows], out_ref.at[rows], gs.at[o, c], gr.at[o, c], {"col": others[o]})

    for c in range(PARTS):
        for o in range(n_col - 1):
            there(o, c).start()
    for c in range(PARTS):
        rows = rows_of(me, c)
        total = part_ref[rows, :].astype(jnp.float32)
        for o in range(n_col - 1):
            there(o, c).wait_recv()
            total = total + inbox[o, pl.ds(c * step, step), :].astype(jnp.float32)
        out_ref[rows, :] = silu_grad(total, up_ref[pl.ds(c * step, step), :])
        for o in range(n_col - 1):
            back(o, c).start()
    for c in range(PARTS):
        for o in range(n_col - 1):
            back(o, c).wait_recv()
    for c in range(PARTS):
        for o in range(n_col - 1):
            there(o, c).wait_send()
            back(o, c).wait_send()


def exchange(partial_value, grad_out, n_col):
    seg, feat_width = grad_out.shape
    dma = pltpu.SemaphoreType.DMA
    return pl.pallas_call(
        functools.partial(exchange_kernel, n_col),
        out_shape=jax.ShapeDtypeStruct(partial_value.shape, jnp.bfloat16),
        in_specs=[VMEM_SPEC] * 2,
        out_specs=VMEM_SPEC,
        scratch_shapes=[pltpu.VMEM((n_col - 1, seg, feat_width), jnp.bfloat16)]
        + [dma((n_col - 1, PARTS))] * 4,
        compiler_params=pltpu.CompilerParams(
            collective_id=1, has_side_effects=True, vmem_limit_bytes=LIMIT
        ),
        name="exchange",
    )(partial_value, grad_out)


def scatter_kernel(
    n_row, n_col, back_ref, fp_hbm, w_ref, gf_ref, gw_ref, fp_ref, xbuf, xown, sbuf, rbuf,
    gsum, gsib_out, gsib_in, gout, gin, gcol, gslice, gfin,
    fsem, ssem, rsem, xs, xr, os, orr, ga, gb_s, gb_r, gc_s, gc_r, gd_s, gd_r, ge,
):
    chips = n_row // 2
    seg = gf_ref.shape[0]
    half = seg // 2
    me = lax.axis_index("row")
    mycol = lax.axis_index("col")
    core = lax.rem(me, 2)
    chip = lax.div(me, 2)
    place = ring_place(chip, chips)
    ways = (1, -1)
    nexts = [row_device(ring_chip(place + way, chips), core) for way in ways]
    sibling = row_device(chip, 1 - core)
    peers = [row_device(lax.rem(chip + o, chips), core) for o in range(1, chips)]
    cols = [{"col": lax.rem(mycol + o, n_col)} for o in range(1, n_col)]
    width = gw_ref.shape[1]
    rows_each = gw_ref.shape[0] // 2 // chips
    load = pltpu.make_async_copy(fp_hbm, fp_ref, fsem)
    load.start()
    greet(peers + [sibling] + cols)
    far = chips // 2
    plans = [
        [(way, far)] + [(h, k) for k in range(far - 1, 0, -1) for h in (1 - way, way)]
        for way in (0, 1)
    ]
    count = len(plans[0])

    def rows_of(owner, h):
        return pl.ds(pl.multiple_of(owner * seg + h * half, half), half)

    def target(way, i):
        h, k = plans[way][i]
        return ring_chip(place + ways[way] * k, chips), h

    def across(way, i):
        to, h = target(way, i)
        return remote(
            back_ref.at[rows_of(to * 2 + 1 - core, h)], xbuf.at[way, i], xs.at[way, i], xr.at[way, i], sibling
        )

    def own_across(h):
        return remote(
            back_ref.at[rows_of(chip * 2 + 1 - core, h)], xown.at[h], os.at[h], orr.at[h], sibling
        )

    def hop(way, i):
        return remote(sbuf.at[way, i], rbuf.at[way, i], ssem.at[way, i], rsem.at[way, i], nexts[way])

    def step(way, i):
        to, h = target(way, i)
        across(way, i).wait_recv()
        total = back_ref[rows_of(to * 2 + core, h), :].astype(jnp.float32) + xbuf[way, i].astype(jnp.float32)
        if i >= 2:
            hop(way, i - 2).wait_recv()
            total = total + rbuf[way, i - 2].astype(jnp.float32)
        sbuf[way, i] = total.astype(sbuf.dtype)
        hop(way, i).start()

    for i in range(count):
        for way in (0, 1):
            across(way, i).start()
    for h in (0, 1):
        own_across(h).start()
    for i in (0, 1):
        for way in (0, 1):
            step(way, i)

    load.wait()
    gsum[...] = jnp.zeros_like(gsum)

    @pl.loop(0, n_row)
    def _(block):
        rows = pl.ds(pl.multiple_of(block * seg, seg), seg)
        gsum[...] += lax.dot_general(
            fp_ref[rows, :], back_ref[rows, :], (((0,), (0,)), ((), ())), preferred_element_type=jnp.float32
        )

    own_rows = gw_ref.shape[0] // 2

    def half_rows(which):
        return pl.ds(pl.multiple_of(which * own_rows, own_rows), own_rows)

    gsib_out[...] = gsum[half_rows(1 - core), :].astype(gsib_out.dtype)
    sib_copy = remote(gsib_out, gsib_in, ga.at[0], ga.at[1], sibling)
    sib_copy.start()

    def spread(o):
        return remote(
            gout.at[lax.rem(chip + o, chips)], gin.at[o - 1], gb_s.at[o - 1], gb_r.at[o - 1], peers[o - 1]
        )

    def stage_b():
        sib_copy.wait_recv()
        total = gsum[half_rows(core), :] + gsib_in[...].astype(jnp.float32)
        gsum[half_rows(core), :] = total
        gout[...] = total.astype(gout.dtype).reshape(gout.shape)
        for o in range(1, chips):
            spread(o).start()

    def over_cols(o):
        return remote(gslice.at[0], gcol.at[o - 1], gc_s.at[o - 1], gc_r.at[o - 1], cols[o - 1])

    def stage_c():
        mine = pl.multiple_of(core * own_rows + chip * rows_each, rows_each)
        total = gsum[pl.ds(mine, rows_each), :]
        for o in range(1, chips):
            spread(o).wait_recv()
            total = total + gin[o - 1].astype(jnp.float32)
        gslice[0] = total
        for o in range(1, n_col):
            over_cols(o).start()

    def collect(o):
        return remote(gslice.at[1], gfin.at[core, chip], gd_s.at[o - 1], gd_r.at[o - 1], peers[o - 1])

    def stage_d():
        total = gslice[0]
        for o in range(1, n_col):
            over_cols(o).wait_recv()
        ordered = None
        for c in range(n_col):
            term = total
            for o in range(1, n_col):
                term = jnp.where(lax.rem(mycol - o + n_col, n_col) == c, gcol[o - 1], term)
            ordered = term if ordered is None else ordered + term
        gslice[1] = ordered
        gfin[core, chip] = ordered
        for o in range(1, chips):
            collect(o).start()

    last_copy = remote(gfin.at[core], gfin.at[core], ge.at[0], ge.at[1], sibling)

    def stage_e():
        for o in range(1, chips):
            collect(o).wait_recv()
        last_copy.start()

    stages = {2: stage_b, 4: stage_c, 5: stage_d}
    for i in range(2, count):
        for way in (0, 1):
            step(way, i)
        if i in stages:
            stages[i]()
    for h in (0, 1):
        own_across(h).wait_recv()
    stage_e()
    order = [count - 2, count - 1]
    for h in (1, 0):
        total = back_ref[rows_of(me, h), :].astype(jnp.float32) + xown[h].astype(jnp.float32)
        for way in (0, 1):
            for i in order:
                if plans[way][i][0] == h:
                    hop(way, i).wait_recv()
                    total = total + rbuf[way, i].astype(jnp.float32)
        gf_ref[pl.ds(h * half, half), :] = lax.dot_general(
            total.astype(jnp.bfloat16), w_ref[...], (((1,), (1,)), ((), ())), preferred_element_type=jnp.float32
        ).astype(gf_ref.dtype)
    last_copy.wait_recv()
    gw_ref[...] = gfin[...].reshape(gw_ref.shape)
    for way in (0, 1):
        for i in range(count):
            hop(way, i).wait_send()
            across(way, i).wait_send()
    for h in (0, 1):
        own_across(h).wait_send()
    sib_copy.wait_send()
    for o in range(1, chips):
        spread(o).wait_send()
        collect(o).wait_send()
    for o in range(1, n_col):
        over_cols(o).wait_send()
    last_copy.wait_send()


def scatter_sum(back_terms, feature_panel, weight, n_row, n_col):
    rows, feat_width = back_terms.shape
    seg = rows // n_row
    half = seg // 2
    chips = n_row // 2
    count = chips - 1
    in_width, out_width = weight.shape
    each = in_width // 2 // chips
    dma = pltpu.SemaphoreType.DMA
    bf16, f32 = jnp.bfloat16, jnp.float32
    return pl.pallas_call(
        functools.partial(scatter_kernel, n_row, n_col),
        out_shape=(
            jax.ShapeDtypeStruct((seg, in_width), bf16),
            jax.ShapeDtypeStruct((in_width, out_width), f32),
        ),
        in_specs=[VMEM_SPEC, pl.BlockSpec(memory_space=pl.ANY), VMEM_SPEC],
        out_specs=(VMEM_SPEC, VMEM_SPEC),
        scratch_shapes=[
            pltpu.VMEM(feature_panel.shape, bf16),
            pltpu.VMEM((2, count, half, feat_width), bf16),
            pltpu.VMEM((2, half, feat_width), bf16),
            pltpu.VMEM((2, count, half, feat_width), bf16),
            pltpu.VMEM((2, count, half, feat_width), bf16),
            pltpu.VMEM((in_width, out_width), f32),
            pltpu.VMEM((in_width // 2, out_width), bf16),
            pltpu.VMEM((in_width // 2, out_width), bf16),
            pltpu.VMEM((chips, each, out_width), bf16),
            pltpu.VMEM((chips - 1, each, out_width), bf16),
            pltpu.VMEM((n_col - 1, each, out_width), f32),
            pltpu.VMEM((2, each, out_width), f32),
            pltpu.VMEM((2, chips, each, out_width), f32),
            dma,
            dma((2, count)),
            dma((2, count)),
            dma((2, count)),
            dma((2, count)),
            dma((2,)),
            dma((2,)),
            dma((2,)),
            dma((chips - 1,)),
            dma((chips - 1,)),
            dma((n_col - 1,)),
            dma((n_col - 1,)),
            dma((chips - 1,)),
            dma((chips - 1,)),
            dma((2,)),
        ],
        compiler_params=pltpu.CompilerParams(
            collective_id=2, has_side_effects=True, vmem_limit_bytes=LIMIT
        ),
        name="scatter",
    )(back_terms, feature_panel, weight)


def spread_kernel(transpose, read_ids, write_ids, count_ref, tiles_hbm, panel_ref, out_ref, buf, acc, sems):
    slots, tile_size, _ = tiles_hbm.shape
    out_tiles = out_ref.shape[0] // tile_size
    chunks = slots // CHUNK
    count = count_ref[0]
    live_chunks = (count + CHUNK - 1) // CHUNK

    def fetch(chunk):
        part = pl.ds(chunk * CHUNK, CHUNK)
        return pltpu.make_async_copy(tiles_hbm.at[part], buf.at[part], sems.at[chunk])

    for chunk in range(chunks):

        @pl.when(chunk < live_chunks)
        def _():
            fetch(chunk).start()

    acc[...] = jnp.zeros_like(acc)
    contract = (((0,), (0,)), ((), ())) if transpose else (((1,), (0,)), ((), ()))

    def one(slot, keep):
        src = pl.multiple_of(read_ids[slot] * tile_size, tile_size)
        product = lax.dot_general(
            buf[slot], panel_ref[pl.ds(src, tile_size), :], contract, preferred_element_type=jnp.float32
        )
        return jnp.where(keep, product, 0.0) if keep is not None else product

    def add(slot, product):
        dst = pl.multiple_of(write_ids[slot] * tile_size, tile_size)
        acc[pl.ds(dst, tile_size), :] += product

    def chunk_step(chunk, carry):
        fetch(chunk).wait()
        base = chunk * CHUNK
        groups = jnp.minimum(count - base, CHUNK) // GROUP

        def group_step(group, carry):
            first = base + group * GROUP
            products = [one(first + k, None) for k in range(GROUP)]
            for k in range(GROUP):
                add(first + k, products[k])
            return carry

        lax.fori_loop(0, groups, group_step, 0)

        def tail_step(slot, carry):
            add(slot, one(slot, None))
            return carry

        lax.fori_loop(base + groups * GROUP, jnp.minimum(count, base + CHUNK), tail_step, 0)
        return carry

    lax.fori_loop(0, live_chunks, chunk_step, 0)

    def finish(tile, carry):
        part = pl.ds(pl.multiple_of(tile * tile_size, tile_size), tile_size)
        out_ref[part, :] = acc[part, :].astype(out_ref.dtype)
        return carry

    lax.fori_loop(0, out_tiles, finish, 0)


def spread_tiles(tiles, read_ids, write_ids, count, panel, out_rows, transpose):
    slots, tile_size, _ = tiles.shape
    feat_width = panel.shape[-1]
    return pl.pallas_call(
        functools.partial(spread_kernel, transpose),
        out_shape=jax.ShapeDtypeStruct((out_rows, feat_width), jnp.bfloat16),
        in_specs=[
            pl.BlockSpec(memory_space=pltpu.SMEM),
            pl.BlockSpec(memory_space=pltpu.SMEM),
            pl.BlockSpec(memory_space=pltpu.SMEM),
            pl.BlockSpec(memory_space=pl.ANY),
            pl.BlockSpec(memory_space=pltpu.VMEM),
        ],
        out_specs=pl.BlockSpec(memory_space=pltpu.VMEM),
        scratch_shapes=[
            pltpu.VMEM(tiles.shape, tiles.dtype),
            pltpu.VMEM((out_rows, feat_width), jnp.float32),
            pltpu.SemaphoreType.DMA((slots // CHUNK,)),
        ],
        compiler_params=pltpu.CompilerParams(vmem_limit_bytes=LIMIT),
        name="back" if transpose else "forth",
    )(read_ids, write_ids, count, tiles, panel)


def body(features, grad_out, weight, tiles, tile_row, tile_col, tile_count):
    segment = features.shape[0]
    n_row, n_col = lax.axis_size("row"), lax.axis_size("col")
    feature_panel, panel = gather_mixed(features, weight, n_row)
    partial_value = spread_tiles(tiles, tile_col, tile_row, tile_count, panel, segment * n_col, False)
    grad_block = exchange(partial_value, grad_out, n_col)
    back_terms = spread_tiles(tiles, tile_row, tile_col, tile_count, grad_block, segment * n_row, True)
    return scatter_sum(back_terms, feature_panel, weight, n_row, n_col)


def solution(mesh):
    in_specs = (
        P(("row", "col"), None),
        P(("row", "col"), None),
        P(),
        P(("row", "col"), None, None),
        P(("row", "col")),
        P(("row", "col")),
        P(("row", "col")),
    )
    out_specs = (P(("row", "col"), None), P())
    return jax.shard_map(body, mesh=mesh, in_specs=in_specs, out_specs=out_specs, check_vma=False)
```

```python
import functools

import jax
import jax.numpy as jnp
from jax import lax
from jax.experimental import pallas as pl
from jax.experimental.pallas import tpu as pltpu
from jax.sharding import PartitionSpec as P

GROUP = 8


MESH = pl.DeviceIdType.MESH
VMEM_SPEC = pl.BlockSpec(memory_space=pltpu.VMEM)


def grant(bytes_held):
    return bytes_held + 6 * 1024 * 1024


def silu_grad(preact, upstream):
    sigmoid_z = jax.nn.sigmoid(preact)
    return (upstream.astype(jnp.float32) * sigmoid_z * (1.0 + preact * (1.0 - sigmoid_z))).astype(
        jnp.bfloat16
    )


def ring_place(chip, chips):
    half = lax.div(chip, 2)
    return jnp.where(lax.rem(chip, 2) == 0, half, chips - 1 - half)


def ring_chip(place, chips):
    place = lax.rem(place + 2 * chips, chips)
    return jnp.where(place < chips // 2, 2 * place, 2 * (chips - 1 - place) + 1)


def row_device(chip, core):
    return {"row": chip * 2 + core}


def greet(partners):
    barrier = pltpu.get_barrier_semaphore()
    for partner in partners:
        pl.semaphore_signal(barrier, inc=1, device_id=partner, device_id_type=MESH)
    pl.semaphore_wait(barrier, len(partners))


def remote(src, dst, send_sem, recv_sem, device):
    return pltpu.make_async_remote_copy(
        src_ref=src, dst_ref=dst, send_sem=send_sem, recv_sem=recv_sem, device_id=device, device_id_type=MESH
    )


def pair_plan(read_row, write_row, count, width):
    f32 = jnp.float32
    slots = read_row.shape[1]
    lane = lax.broadcasted_iota(jnp.int32, (slots, slots), 1)
    sub = lax.broadcasted_iota(jnp.int32, (slots, slots), 0)

    def as_column(row):
        return jnp.sum(jnp.where(lane == sub, row, 0.0), axis=1, keepdims=True)

    read_col = as_column(jnp.broadcast_to(read_row.astype(f32), (slots, slots)))
    row = jnp.broadcast_to(write_row.astype(f32), (slots, slots))
    write_col = as_column(row)
    col = jnp.broadcast_to(write_col, (slots, slots))
    live = jnp.where((lane < count) & (sub < count), 1.0, 0.0)
    same = jnp.where(row == col, live, 0.0)
    rank_col = jnp.sum(jnp.where(lane < sub, same, 0.0), axis=1, keepdims=True)
    rank_row = jnp.sum(jnp.where(sub < lane, same, 0.0), axis=0, keepdims=True)
    odd_row = rank_row - 2.0 * jnp.floor(rank_row * 0.5)
    opens = jnp.where(lane < count, 1.0 - jnp.broadcast_to(odd_row, (slots, slots)), 0.0)
    base = jnp.sum(jnp.where(row < col, opens, 0.0), axis=1, keepdims=True)
    pairs = jnp.sum(opens, axis=1, keepdims=True)[0:1, :]
    place = lax.broadcasted_iota(jnp.int32, (slots, width), 1).astype(f32)
    slot = lax.broadcasted_iota(jnp.int32, (slots, width), 0)
    hit = jnp.where(slot < count, jnp.where(place == 2.0 * base + rank_col, 1.0, 0.0), 0.0)
    slot_at = jnp.sum(hit * (slot - slots).astype(f32), axis=0, keepdims=True) + float(slots)
    last = lax.broadcasted_iota(jnp.int32, (1, width), 1) == width - 1
    slot_at = jnp.where(last, jnp.broadcast_to(pairs, (1, width)), slot_at)
    read_at = jnp.sum(hit * read_col, axis=0, keepdims=True)
    write_at = jnp.sum(hit * write_col, axis=0, keepdims=True)
    return [part.astype(jnp.int32) for part in (slot_at, read_at, write_at)]


def gather_kernel(
    n_row, count_ref, f_ref, w_ref, tr_ref, tc_ref, tiles_hbm,
    fp_ref, mp_ref, tiles_ref, forth_ref, back_ref,
    ssem, rsem, xs, xr, os, orr, tsem,
):
    slots = tiles_hbm.shape[0]
    load = pltpu.make_async_copy(tiles_hbm, tiles_ref.at[pl.ds(0, slots)], tsem)
    load.start()
    chips = n_row // 2
    seg = f_ref.shape[0]
    half = seg // 2
    me = lax.axis_index("row")
    core = lax.rem(me, 2)
    chip = lax.div(me, 2)
    place = ring_place(chip, chips)
    ways = (1, -1)
    nexts = [row_device(ring_chip(place + way, chips), core) for way in ways]
    sibling = row_device(chip, 1 - core)
    greet(nexts + [sibling])
    far = chips // 2
    plans = [
        [(h, k) for k in range(1, far) for h in (way, 1 - way)] + [(way, far)] for way in (0, 1)
    ]
    count = len(plans[0])

    def rows_of(owner, h):
        return pl.ds(pl.multiple_of(owner * seg + h * half, half), half)

    def origin(way, k):
        return ring_chip(place - ways[way] * k, chips)

    def hop(way, i):
        h, k = plans[way][i]
        if k == 1:
            src = f_ref.at[pl.ds(h * half, half)]
            rows = rows_of(me, h)
        else:
            rows = rows_of(origin(way, k - 1) * 2 + core, h)
            src = fp_ref.at[rows]
        return remote(src, fp_ref.at[rows], ssem.at[way, i], rsem.at[way, i], nexts[way])

    def across(way, i):
        h, k = plans[way][i]
        rows = rows_of(origin(way, k) * 2 + core, h)
        return remote(fp_ref.at[rows], fp_ref.at[rows], xs.at[way, i], xr.at[way, i], sibling)

    def own_across(h):
        return remote(
            f_ref.at[pl.ds(h * half, half)], fp_ref.at[rows_of(me, h)], os.at[h], orr.at[h], sibling
        )

    def mix(owner, h):
        rows = rows_of(owner, h)
        mp_ref[rows, :] = jnp.dot(
            fp_ref[rows, :], w_ref[...], preferred_element_type=jnp.float32
        ).astype(mp_ref.dtype)

    for i in (0, 1):
        for way in (0, 1):
            hop(way, i).start()
    for h in (0, 1):
        own_across(h).start()
    fp_ref[pl.ds(pl.multiple_of(me * seg, seg), seg), :] = f_ref[...]
    for h in (0, 1):
        mix(me, h)
    tiles_ref[slots] = jnp.zeros_like(tiles_ref[slots])
    tr, tc, live = tr_ref[...], tc_ref[...], count_ref[0]
    for plan_ref, reads, writes in ((forth_ref, tc, tr), (back_ref, tr, tc)):
        for line, part in enumerate(pair_plan(reads, writes, live, plan_ref.shape[1])):
            plan_ref[line : line + 1, :] = part
    for i in range(count):
        for way in (0, 1):
            hop(way, i).wait_recv()
            if i + 2 < count:
                hop(way, i + 2).start()
            across(way, i).start()
        if i == 0:
            for h in (0, 1):
                own_across(h).wait_recv()
                mix(chip * 2 + 1 - core, h)
        for way in (0, 1):
            h, k = plans[way][i]
            mix(origin(way, k) * 2 + core, h)
            if i > 0:
                h, k = plans[way][i - 1]
                across(way, i - 1).wait_recv()
                mix(origin(way, k) * 2 + 1 - core, h)
    for way in (0, 1):
        h, k = plans[way][count - 1]
        across(way, count - 1).wait_recv()
        mix(origin(way, k) * 2 + 1 - core, h)
    for way in (0, 1):
        for i in range(count):
            hop(way, i).wait_send()
            across(way, i).wait_send()
    for h in (0, 1):
        own_across(h).wait_send()
    load.wait()


def gather_mixed(features, weight, tiles, tile_row, tile_col, tile_count, n_row):
    seg, feat_width = features.shape
    count = n_row // 2 - 1
    slots, tile_size, _ = tiles.shape
    shape = jax.ShapeDtypeStruct((n_row * seg, feat_width), features.dtype)
    entries = slots + min(slots, n_row * seg // tile_size) + 2 * GROUP + 1
    plan = jax.ShapeDtypeStruct((3, -(-entries // 128) * 128), jnp.int32)
    held = jax.ShapeDtypeStruct((slots + 1, tile_size, tile_size), tiles.dtype)
    dma = pltpu.SemaphoreType.DMA
    return pl.pallas_call(
        functools.partial(gather_kernel, n_row),
        out_shape=(shape, shape, held, plan, plan),
        in_specs=[pl.BlockSpec(memory_space=pltpu.SMEM)]
        + [VMEM_SPEC] * 4
        + [pl.BlockSpec(memory_space=pltpu.MemorySpace.HBM)],
        out_specs=(VMEM_SPEC,) * 5,
        scratch_shapes=[dma((2, count))] * 4 + [dma((2,))] * 2 + [dma],
        compiler_params=pltpu.CompilerParams(
            collective_id=0,
            has_side_effects=True,
            vmem_limit_bytes=grant(4 * shape.size + 2 * held.size + 2 * features.size),
        ),
        name="gather",
    )(tile_count, features, weight, tile_row.reshape(1, slots), tile_col.reshape(1, slots), tiles)


PARTS = 4


def exchange_kernel(n_col, part_ref, up_ref, out_ref, inbox, ssem, rsem, gs, gr):
    seg = up_ref.shape[0]
    step = seg // PARTS
    me = lax.axis_index("col")
    others = [lax.rem(me + o, n_col) for o in range(1, n_col)]
    greet([{"col": other} for other in others])

    def rows_of(owner, c):
        return pl.ds(pl.multiple_of(owner * seg + c * step, step), step)

    def there(o, c):
        return remote(
            part_ref.at[rows_of(others[o], c)],
            inbox.at[o, pl.ds(c * step, step)],
            ssem.at[o, c],
            rsem.at[o, c],
            {"col": others[o]},
        )

    def back(o, c):
        rows = rows_of(me, c)
        return remote(out_ref.at[rows], out_ref.at[rows], gs.at[o, c], gr.at[o, c], {"col": others[o]})

    for c in range(PARTS):
        for o in range(n_col - 1):
            there(o, c).start()
    for c in range(PARTS):
        rows = rows_of(me, c)
        total = part_ref[rows, :].astype(jnp.float32)
        for o in range(n_col - 1):
            there(o, c).wait_recv()
            total = total + inbox[o, pl.ds(c * step, step), :].astype(jnp.float32)
        out_ref[rows, :] = silu_grad(total, up_ref[pl.ds(c * step, step), :])
        for o in range(n_col - 1):
            back(o, c).start()
    for c in range(PARTS):
        for o in range(n_col - 1):
            back(o, c).wait_recv()
    for c in range(PARTS):
        for o in range(n_col - 1):
            there(o, c).wait_send()
            back(o, c).wait_send()


def exchange(partial_value, grad_out, n_col):
    seg, feat_width = grad_out.shape
    dma = pltpu.SemaphoreType.DMA
    return pl.pallas_call(
        functools.partial(exchange_kernel, n_col),
        out_shape=jax.ShapeDtypeStruct(partial_value.shape, jnp.bfloat16),
        in_specs=[VMEM_SPEC] * 2,
        out_specs=VMEM_SPEC,
        scratch_shapes=[pltpu.VMEM((n_col - 1, seg, feat_width), jnp.bfloat16)]
        + [dma((n_col - 1, PARTS))] * 4,
        compiler_params=pltpu.CompilerParams(
            collective_id=1, has_side_effects=True, vmem_limit_bytes=grant(6 * partial_value.size)
        ),
        name="exchange",
    )(partial_value, grad_out)


def scatter_kernel(
    n_row, n_col, back_ref, fp_ref, w_ref, gf_ref, gw_ref, xbuf, xown, sbuf, rbuf,
    gsum, gsib_out, gsib_in, gout, gin, gcol, gslice, gfin,
    ssem, rsem, xs, xr, os, orr, ga, gb_s, gb_r, gc_s, gc_r, gd_s, gd_r, ge,
):
    chips = n_row // 2
    seg = gf_ref.shape[0]
    half = seg // 2
    me = lax.axis_index("row")
    mycol = lax.axis_index("col")
    core = lax.rem(me, 2)
    chip = lax.div(me, 2)
    place = ring_place(chip, chips)
    ways = (1, -1)
    nexts = [row_device(ring_chip(place + way, chips), core) for way in ways]
    sibling = row_device(chip, 1 - core)
    peers = [row_device(lax.rem(chip + o, chips), core) for o in range(1, chips)]
    cols = [{"col": lax.rem(mycol + o, n_col)} for o in range(1, n_col)]
    width = gw_ref.shape[1]
    rows_each = gw_ref.shape[0] // 2 // chips
    greet(peers + [sibling] + cols)
    far = chips // 2
    plans = [
        [(way, far)] + [(h, k) for k in range(far - 1, 0, -1) for h in (1 - way, way)]
        for way in (0, 1)
    ]
    count = len(plans[0])

    def rows_of(owner, h):
        return pl.ds(pl.multiple_of(owner * seg + h * half, half), half)

    def target(way, i):
        h, k = plans[way][i]
        return ring_chip(place + ways[way] * k, chips), h

    def across(way, i):
        to, h = target(way, i)
        return remote(
            back_ref.at[rows_of(to * 2 + 1 - core, h)], xbuf.at[way, i], xs.at[way, i], xr.at[way, i], sibling
        )

    def own_across(h):
        return remote(
            back_ref.at[rows_of(chip * 2 + 1 - core, h)], xown.at[h], os.at[h], orr.at[h], sibling
        )

    def hop(way, i):
        return remote(sbuf.at[way, i], rbuf.at[way, i], ssem.at[way, i], rsem.at[way, i], nexts[way])

    def step(way, i):
        to, h = target(way, i)
        across(way, i).wait_recv()
        total = back_ref[rows_of(to * 2 + core, h), :].astype(jnp.float32) + xbuf[way, i].astype(jnp.float32)
        if i >= 2:
            hop(way, i - 2).wait_recv()
            total = total + rbuf[way, i - 2].astype(jnp.float32)
        sbuf[way, i] = total.astype(sbuf.dtype)
        hop(way, i).start()

    for i in range(count):
        for way in (0, 1):
            across(way, i).start()
    for h in (0, 1):
        own_across(h).start()
    for i in (0, 1):
        for way in (0, 1):
            step(way, i)

    gsum[...] = jnp.zeros_like(gsum)

    @pl.loop(0, n_row)
    def _(block):
        rows = pl.ds(pl.multiple_of(block * seg, seg), seg)
        gsum[...] += lax.dot_general(
            fp_ref[rows, :], back_ref[rows, :], (((0,), (0,)), ((), ())), preferred_element_type=jnp.float32
        )

    own_rows = gw_ref.shape[0] // 2

    def half_rows(which):
        return pl.ds(pl.multiple_of(which * own_rows, own_rows), own_rows)

    gsib_out[...] = gsum[half_rows(1 - core), :].astype(gsib_out.dtype)
    sib_copy = remote(gsib_out, gsib_in, ga.at[0], ga.at[1], sibling)
    sib_copy.start()

    def spread(o):
        return remote(
            gout.at[lax.rem(chip + o, chips)], gin.at[o - 1], gb_s.at[o - 1], gb_r.at[o - 1], peers[o - 1]
        )

    def stage_b():
        sib_copy.wait_recv()
        total = gsum[half_rows(core), :] + gsib_in[...].astype(jnp.float32)
        gsum[half_rows(core), :] = total
        gout[...] = total.astype(gout.dtype).reshape(gout.shape)
        for o in range(1, chips):
            spread(o).start()

    def over_cols(o):
        return remote(gslice.at[0], gcol.at[o - 1], gc_s.at[o - 1], gc_r.at[o - 1], cols[o - 1])

    def stage_c():
        mine = pl.multiple_of(core * own_rows + chip * rows_each, rows_each)
        total = gsum[pl.ds(mine, rows_each), :]
        for o in range(1, chips):
            spread(o).wait_recv()
            total = total + gin[o - 1].astype(jnp.float32)
        gslice[0] = total
        for o in range(1, n_col):
            over_cols(o).start()

    def collect(o):
        return remote(gslice.at[1], gfin.at[core, chip], gd_s.at[o - 1], gd_r.at[o - 1], peers[o - 1])

    def stage_d():
        total = gslice[0]
        for o in range(1, n_col):
            over_cols(o).wait_recv()
        ordered = None
        for c in range(n_col):
            term = total
            for o in range(1, n_col):
                term = jnp.where(lax.rem(mycol - o + n_col, n_col) == c, gcol[o - 1], term)
            ordered = term if ordered is None else ordered + term
        gslice[1] = ordered
        gfin[core, chip] = ordered
        for o in range(1, chips):
            collect(o).start()

    last_copy = remote(gfin.at[core], gfin.at[core], ge.at[0], ge.at[1], sibling)

    def stage_e():
        for o in range(1, chips):
            collect(o).wait_recv()
        last_copy.start()

    stages = {2: stage_b, 4: stage_c, 5: stage_d}
    for i in range(2, count):
        for way in (0, 1):
            step(way, i)
        if i in stages:
            stages[i]()
    for h in (0, 1):
        own_across(h).wait_recv()
    stage_e()
    order = [count - 2, count - 1]
    for h in (1, 0):
        total = back_ref[rows_of(me, h), :].astype(jnp.float32) + xown[h].astype(jnp.float32)
        for way in (0, 1):
            for i in order:
                if plans[way][i][0] == h:
                    hop(way, i).wait_recv()
                    total = total + rbuf[way, i].astype(jnp.float32)
        gf_ref[pl.ds(h * half, half), :] = lax.dot_general(
            total.astype(jnp.bfloat16), w_ref[...], (((1,), (1,)), ((), ())), preferred_element_type=jnp.float32
        ).astype(gf_ref.dtype)
    last_copy.wait_recv()
    gw_ref[...] = gfin[...].reshape(gw_ref.shape)
    for way in (0, 1):
        for i in range(count):
            hop(way, i).wait_send()
            across(way, i).wait_send()
    for h in (0, 1):
        own_across(h).wait_send()
    sib_copy.wait_send()
    for o in range(1, chips):
        spread(o).wait_send()
        collect(o).wait_send()
    for o in range(1, n_col):
        over_cols(o).wait_send()
    last_copy.wait_send()


def scatter_sum(back_terms, feature_panel, weight, n_row, n_col):
    rows, feat_width = back_terms.shape
    seg = rows // n_row
    half = seg // 2
    chips = n_row // 2
    count = chips - 1
    in_width, out_width = weight.shape
    each = in_width // 2 // chips
    dma = pltpu.SemaphoreType.DMA
    bf16, f32 = jnp.bfloat16, jnp.float32
    return pl.pallas_call(
        functools.partial(scatter_kernel, n_row, n_col),
        out_shape=(
            jax.ShapeDtypeStruct((seg, in_width), bf16),
            jax.ShapeDtypeStruct((in_width, out_width), f32),
        ),
        in_specs=[VMEM_SPEC] * 3,
        out_specs=(VMEM_SPEC, VMEM_SPEC),
        scratch_shapes=[
            pltpu.VMEM((2, count, half, feat_width), bf16),
            pltpu.VMEM((2, half, feat_width), bf16),
            pltpu.VMEM((2, count, half, feat_width), bf16),
            pltpu.VMEM((2, count, half, feat_width), bf16),
            pltpu.VMEM((in_width, out_width), f32),
            pltpu.VMEM((in_width // 2, out_width), bf16),
            pltpu.VMEM((in_width // 2, out_width), bf16),
            pltpu.VMEM((chips, each, out_width), bf16),
            pltpu.VMEM((chips - 1, each, out_width), bf16),
            pltpu.VMEM((n_col - 1, each, out_width), f32),
            pltpu.VMEM((2, each, out_width), f32),
            pltpu.VMEM((2, chips, each, out_width), f32),
            dma((2, count)),
            dma((2, count)),
            dma((2, count)),
            dma((2, count)),
            dma((2,)),
            dma((2,)),
            dma((2,)),
            dma((chips - 1,)),
            dma((chips - 1,)),
            dma((n_col - 1,)),
            dma((n_col - 1,)),
            dma((chips - 1,)),
            dma((chips - 1,)),
            dma((2,)),
        ],
        compiler_params=pltpu.CompilerParams(
            collective_id=2, has_side_effects=True, vmem_limit_bytes=grant(10 * back_terms.size)
        ),
        name="scatter",
    )(back_terms, feature_panel, weight)


def spread_kernel(transpose, plan_ref, tiles_ref, panel_ref, out_ref, acc):
    tile_size = tiles_ref.shape[1]
    out_tiles = out_ref.shape[0] // tile_size
    pairs = plan_ref[0, plan_ref.shape[1] - 1]
    acc[...] = jnp.zeros_like(acc)
    contract = (((0,), (0,)), ((), ())) if transpose else (((1,), (0,)), ((), ()))

    def read_rows(entry):
        return panel_ref[pl.ds(pl.multiple_of(plan_ref[1, entry] * tile_size, tile_size), tile_size), :]

    def product(pair):
        entries = (2 * pair, 2 * pair + 1)
        left = jnp.concatenate([tiles_ref[plan_ref[0, e]] for e in entries], axis=0 if transpose else 1)
        right = jnp.concatenate([read_rows(e) for e in entries], axis=0)
        return lax.dot_general(left, right, contract, preferred_element_type=jnp.float32)

    def add(pair, value):
        dst = pl.multiple_of(plan_ref[2, 2 * pair] * tile_size, tile_size)
        acc[pl.ds(dst, tile_size), :] += value

    def group_step(group, carry):
        first = group * GROUP
        values = [product(first + k) for k in range(GROUP)]
        for k in range(GROUP):
            add(first + k, values[k])
        return carry

    lax.fori_loop(0, (pairs + GROUP - 1) // GROUP, group_step, 0)

    def finish(tile, carry):
        part = pl.ds(pl.multiple_of(tile * tile_size, tile_size), tile_size)
        out_ref[part, :] = acc[part, :].astype(out_ref.dtype)
        return carry

    lax.fori_loop(0, out_tiles, finish, 0)


def spread_tiles(tiles, plan, panel, out_rows, transpose):
    feat_width = panel.shape[-1]
    return pl.pallas_call(
        functools.partial(spread_kernel, transpose),
        out_shape=jax.ShapeDtypeStruct((out_rows, feat_width), jnp.bfloat16),
        in_specs=[pl.BlockSpec(memory_space=pltpu.SMEM), VMEM_SPEC, VMEM_SPEC],
        out_specs=VMEM_SPEC,
        scratch_shapes=[pltpu.VMEM((out_rows, feat_width), jnp.float32)],
        compiler_params=pltpu.CompilerParams(
            vmem_limit_bytes=grant(2 * tiles.size + 2 * panel.size + 6 * out_rows * feat_width)
        ),
        name="back" if transpose else "forth",
    )(plan, tiles, panel)


def finish_kernel(a_ref, b_ref, a_out, b_out, sems):
    copies = [
        pltpu.make_async_copy(a_ref, a_out, sems.at[0]),
        pltpu.make_async_copy(b_ref, b_out, sems.at[1]),
    ]
    for copy in copies:
        copy.start()
    for copy in copies:
        copy.wait()


def finish(a, b):
    hbm = pl.BlockSpec(memory_space=pltpu.MemorySpace.HBM)
    return pl.pallas_call(
        finish_kernel,
        out_shape=(jax.ShapeDtypeStruct(a.shape, a.dtype), jax.ShapeDtypeStruct(b.shape, b.dtype)),
        in_specs=[VMEM_SPEC] * 2,
        out_specs=(hbm, hbm),
        scratch_shapes=[pltpu.SemaphoreType.DMA((2,))],
        compiler_params=pltpu.CompilerParams(vmem_limit_bytes=grant(2 * a.size + 4 * b.size)),
        name="finish",
    )(a, b)


def body(features, grad_out, weight, tiles, tile_row, tile_col, tile_count):
    segment = features.shape[0]
    n_row, n_col = lax.axis_size("row"), lax.axis_size("col")
    feature_panel, panel, held, forth_plan, back_plan = gather_mixed(
        features, weight, tiles, tile_row, tile_col, tile_count, n_row
    )
    partial_value = spread_tiles(held, forth_plan, panel, segment * n_col, False)
    grad_block = exchange(partial_value, grad_out, n_col)
    back_terms = spread_tiles(held, back_plan, grad_block, segment * n_row, True)
    return finish(*scatter_sum(back_terms, feature_panel, weight, n_row, n_col))


def solution(mesh):
    in_specs = (
        P(("row", "col"), None),
        P(("row", "col"), None),
        P(),
        P(("row", "col"), None, None),
        P(("row", "col")),
        P(("row", "col")),
        P(("row", "col")),
    )
    out_specs = (P(("row", "col"), None), P())
    return jax.shard_map(body, mesh=mesh, in_specs=in_specs, out_specs=out_specs, check_vma=False)
```

```python
import functools

import jax
import jax.numpy as jnp
from jax import lax
from jax.experimental import pallas as pl
from jax.experimental.pallas import tpu as pltpu
from jax.sharding import PartitionSpec as P

GROUP = 8


MESH = pl.DeviceIdType.MESH
VMEM_SPEC = pl.BlockSpec(memory_space=pltpu.VMEM)


def grant(bytes_held):
    return bytes_held + 6 * 1024 * 1024


def silu_grad(preact, upstream):
    sigmoid_z = jax.nn.sigmoid(preact)
    return (upstream.astype(jnp.float32) * sigmoid_z * (1.0 + preact * (1.0 - sigmoid_z))).astype(
        jnp.bfloat16
    )


def ring_place(chip, chips):
    half = lax.div(chip, 2)
    return jnp.where(lax.rem(chip, 2) == 0, half, chips - 1 - half)


def ring_chip(place, chips):
    place = lax.rem(place + 2 * chips, chips)
    return jnp.where(place < chips // 2, 2 * place, 2 * (chips - 1 - place) + 1)


def row_device(chip, core):
    return {"row": chip * 2 + core}


def greet(partners):
    barrier = pltpu.get_barrier_semaphore()
    for partner in partners:
        pl.semaphore_signal(barrier, inc=1, device_id=partner, device_id_type=MESH)
    pl.semaphore_wait(barrier, len(partners))


def remote(src, dst, send_sem, recv_sem, device):
    return pltpu.make_async_remote_copy(
        src_ref=src, dst_ref=dst, send_sem=send_sem, recv_sem=recv_sem, device_id=device, device_id_type=MESH
    )


def pair_plan(read_row, write_row, count, width):
    f32 = jnp.float32
    slots = read_row.shape[1]
    lane = lax.broadcasted_iota(jnp.int32, (slots, slots), 1)
    sub = lax.broadcasted_iota(jnp.int32, (slots, slots), 0)

    def as_column(row):
        return jnp.sum(jnp.where(lane == sub, row, 0.0), axis=1, keepdims=True)

    read_col = as_column(jnp.broadcast_to(read_row.astype(f32), (slots, slots)))
    row = jnp.broadcast_to(write_row.astype(f32), (slots, slots))
    write_col = as_column(row)
    col = jnp.broadcast_to(write_col, (slots, slots))
    live = jnp.where((lane < count) & (sub < count), 1.0, 0.0)
    same = jnp.where(row == col, live, 0.0)
    rank_col = jnp.sum(jnp.where(lane < sub, same, 0.0), axis=1, keepdims=True)
    rank_row = jnp.sum(jnp.where(sub < lane, same, 0.0), axis=0, keepdims=True)
    odd_row = rank_row - 2.0 * jnp.floor(rank_row * 0.5)
    opens = jnp.where(lane < count, 1.0 - jnp.broadcast_to(odd_row, (slots, slots)), 0.0)
    base = jnp.sum(jnp.where(row < col, opens, 0.0), axis=1, keepdims=True)
    pairs = jnp.sum(opens, axis=1, keepdims=True)[0:1, :]
    place = lax.broadcasted_iota(jnp.int32, (slots, width), 1).astype(f32)
    slot = lax.broadcasted_iota(jnp.int32, (slots, width), 0)
    hit = jnp.where(slot < count, jnp.where(place == 2.0 * base + rank_col, 1.0, 0.0), 0.0)
    slot_at = jnp.sum(hit * (slot - slots).astype(f32), axis=0, keepdims=True) + float(slots)
    last = lax.broadcasted_iota(jnp.int32, (1, width), 1) == width - 1
    slot_at = jnp.where(last, jnp.broadcast_to(pairs, (1, width)), slot_at)
    read_at = jnp.sum(hit * read_col, axis=0, keepdims=True)
    write_at = jnp.sum(hit * write_col, axis=0, keepdims=True)
    return [part.astype(jnp.int32) for part in (slot_at, read_at, write_at)]


def gather_kernel(
    n_row, count_ref, f_hbm, w_hbm, tr_hbm, tc_hbm, tiles_hbm,
    fp_ref, mp_ref, tiles_ref, forth_ref, back_ref,
    f_ref, w_ref, tr_ref, tc_ref, ssem, rsem, xs, xr, os, orr, tsem, isem,
):
    inputs = [
        pltpu.make_async_copy(src, dst, isem.at[at])
        for at, (src, dst) in enumerate(
            ((f_hbm, f_ref), (w_hbm, w_ref), (tr_hbm, tr_ref), (tc_hbm, tc_ref))
        )
    ]
    for copy in inputs:
        copy.start()
    slots = tiles_hbm.shape[0]
    load = pltpu.make_async_copy(tiles_hbm, tiles_ref.at[pl.ds(0, slots)], tsem)
    load.start()
    chips = n_row // 2
    seg = f_ref.shape[0]
    half = seg // 2
    me = lax.axis_index("row")
    core = lax.rem(me, 2)
    chip = lax.div(me, 2)
    place = ring_place(chip, chips)
    ways = (1, -1)
    nexts = [row_device(ring_chip(place + way, chips), core) for way in ways]
    sibling = row_device(chip, 1 - core)
    greet(nexts + [sibling])
    inputs[0].wait()
    far = chips // 2
    plans = [
        [(h, k) for k in range(1, far) for h in (way, 1 - way)] + [(way, far)] for way in (0, 1)
    ]
    count = len(plans[0])

    def rows_of(owner, h):
        return pl.ds(pl.multiple_of(owner * seg + h * half, half), half)

    def origin(way, k):
        return ring_chip(place - ways[way] * k, chips)

    def hop(way, i):
        h, k = plans[way][i]
        if k == 1:
            src = f_ref.at[pl.ds(h * half, half)]
            rows = rows_of(me, h)
        else:
            rows = rows_of(origin(way, k - 1) * 2 + core, h)
            src = fp_ref.at[rows]
        return remote(src, fp_ref.at[rows], ssem.at[way, i], rsem.at[way, i], nexts[way])

    def across(way, i):
        h, k = plans[way][i]
        rows = rows_of(origin(way, k) * 2 + core, h)
        return remote(fp_ref.at[rows], fp_ref.at[rows], xs.at[way, i], xr.at[way, i], sibling)

    def own_across(h):
        return remote(
            f_ref.at[pl.ds(h * half, half)], fp_ref.at[rows_of(me, h)], os.at[h], orr.at[h], sibling
        )

    def mix(owner, h):
        rows = rows_of(owner, h)
        mp_ref[rows, :] = jnp.dot(
            fp_ref[rows, :], w_ref[...], preferred_element_type=jnp.float32
        ).astype(mp_ref.dtype)

    for i in (0, 1):
        for way in (0, 1):
            hop(way, i).start()
    for h in (0, 1):
        own_across(h).start()
    for copy in inputs[1:]:
        copy.wait()
    fp_ref[pl.ds(pl.multiple_of(me * seg, seg), seg), :] = f_ref[...]
    for h in (0, 1):
        mix(me, h)
    tiles_ref[slots] = jnp.zeros_like(tiles_ref[slots])
    tr, tc, live = tr_ref[...], tc_ref[...], count_ref[0]
    for plan_ref, reads, writes in ((forth_ref, tc, tr), (back_ref, tr, tc)):
        for line, part in enumerate(pair_plan(reads, writes, live, plan_ref.shape[1])):
            plan_ref[line : line + 1, :] = part
    for i in range(count):
        for way in (0, 1):
            hop(way, i).wait_recv()
            if i + 2 < count:
                hop(way, i + 2).start()
            across(way, i).start()
        if i == 0:
            for h in (0, 1):
                own_across(h).wait_recv()
                mix(chip * 2 + 1 - core, h)
        for way in (0, 1):
            h, k = plans[way][i]
            mix(origin(way, k) * 2 + core, h)
            if i > 0:
                h, k = plans[way][i - 1]
                across(way, i - 1).wait_recv()
                mix(origin(way, k) * 2 + 1 - core, h)
    for way in (0, 1):
        h, k = plans[way][count - 1]
        across(way, count - 1).wait_recv()
        mix(origin(way, k) * 2 + 1 - core, h)
    for way in (0, 1):
        for i in range(count):
            hop(way, i).wait_send()
            across(way, i).wait_send()
    for h in (0, 1):
        own_across(h).wait_send()
    load.wait()


def gather_mixed(features, weight, tiles, tile_row, tile_col, tile_count, n_row):
    seg, feat_width = features.shape
    count = n_row // 2 - 1
    slots, tile_size, _ = tiles.shape
    shape = jax.ShapeDtypeStruct((n_row * seg, feat_width), features.dtype)
    entries = slots + min(slots, n_row * seg // tile_size) + 2 * GROUP + 1
    plan = jax.ShapeDtypeStruct((3, -(-entries // 128) * 128), jnp.int32)
    held = jax.ShapeDtypeStruct((slots + 1, tile_size, tile_size), tiles.dtype)
    dma = pltpu.SemaphoreType.DMA
    return pl.pallas_call(
        functools.partial(gather_kernel, n_row),
        out_shape=(shape, shape, held, plan, plan),
        in_specs=[pl.BlockSpec(memory_space=pltpu.SMEM)]
        + [pl.BlockSpec(memory_space=pltpu.MemorySpace.HBM)] * 5,
        out_specs=(VMEM_SPEC,) * 5,
        scratch_shapes=[
            pltpu.VMEM(features.shape, features.dtype),
            pltpu.VMEM(weight.shape, weight.dtype),
            pltpu.VMEM((1, slots), jnp.int32),
            pltpu.VMEM((1, slots), jnp.int32),
        ]
        + [dma((2, count))] * 4
        + [dma((2,))] * 2
        + [dma, dma((4,))],
        compiler_params=pltpu.CompilerParams(
            collective_id=0,
            has_side_effects=True,
            vmem_limit_bytes=grant(4 * shape.size + 2 * held.size + 2 * features.size),
        ),
        name="gather",
    )(
        tile_count,
        *(
            pltpu.with_memory_space_constraint(array, pltpu.MemorySpace.HBM)
            for array in (
                features, weight, tile_row.reshape(1, slots), tile_col.reshape(1, slots), tiles
            )
        ),
    )


PARTS = 4


def exchange_kernel(n_col, part_ref, up_ref, out_ref, inbox, ssem, rsem, gs, gr):
    seg = up_ref.shape[0]
    step = seg // PARTS
    me = lax.axis_index("col")
    others = [lax.rem(me + o, n_col) for o in range(1, n_col)]
    greet([{"col": other} for other in others])

    def rows_of(owner, c):
        return pl.ds(pl.multiple_of(owner * seg + c * step, step), step)

    def there(o, c):
        return remote(
            part_ref.at[rows_of(others[o], c)],
            inbox.at[o, pl.ds(c * step, step)],
            ssem.at[o, c],
            rsem.at[o, c],
            {"col": others[o]},
        )

    def back(o, c):
        rows = rows_of(me, c)
        return remote(out_ref.at[rows], out_ref.at[rows], gs.at[o, c], gr.at[o, c], {"col": others[o]})

    for c in range(PARTS):
        for o in range(n_col - 1):
            there(o, c).start()
    for c in range(PARTS):
        rows = rows_of(me, c)
        total = part_ref[rows, :].astype(jnp.float32)
        for o in range(n_col - 1):
            there(o, c).wait_recv()
            total = total + inbox[o, pl.ds(c * step, step), :].astype(jnp.float32)
        out_ref[rows, :] = silu_grad(total, up_ref[pl.ds(c * step, step), :])
        for o in range(n_col - 1):
            back(o, c).start()
    for c in range(PARTS):
        for o in range(n_col - 1):
            back(o, c).wait_recv()
    for c in range(PARTS):
        for o in range(n_col - 1):
            there(o, c).wait_send()
            back(o, c).wait_send()


def exchange(partial_value, grad_out, n_col):
    seg, feat_width = grad_out.shape
    dma = pltpu.SemaphoreType.DMA
    return pl.pallas_call(
        functools.partial(exchange_kernel, n_col),
        out_shape=jax.ShapeDtypeStruct(partial_value.shape, jnp.bfloat16),
        in_specs=[VMEM_SPEC] * 2,
        out_specs=VMEM_SPEC,
        scratch_shapes=[pltpu.VMEM((n_col - 1, seg, feat_width), jnp.bfloat16)]
        + [dma((n_col - 1, PARTS))] * 4,
        compiler_params=pltpu.CompilerParams(
            collective_id=1, has_side_effects=True, vmem_limit_bytes=grant(6 * partial_value.size)
        ),
        name="exchange",
    )(partial_value, grad_out)


def scatter_kernel(
    n_row, n_col, back_ref, fp_ref, w_ref, gf_ref, gw_ref, xbuf, xown, sbuf, rbuf,
    gsum, gsib_out, gsib_in, gout, gin, gcol, gslice, gfin,
    ssem, rsem, xs, xr, os, orr, ga, gb_s, gb_r, gc_s, gc_r, gd_s, gd_r, ge,
):
    chips = n_row // 2
    seg = gf_ref.shape[0]
    half = seg // 2
    me = lax.axis_index("row")
    mycol = lax.axis_index("col")
    core = lax.rem(me, 2)
    chip = lax.div(me, 2)
    place = ring_place(chip, chips)
    ways = (1, -1)
    nexts = [row_device(ring_chip(place + way, chips), core) for way in ways]
    sibling = row_device(chip, 1 - core)
    peers = [row_device(lax.rem(chip + o, chips), core) for o in range(1, chips)]
    cols = [{"col": lax.rem(mycol + o, n_col)} for o in range(1, n_col)]
    width = gw_ref.shape[1]
    rows_each = gw_ref.shape[0] // 2 // chips
    greet(peers + [sibling] + cols)
    far = chips // 2
    plans = [
        [(way, far)] + [(h, k) for k in range(far - 1, 0, -1) for h in (1 - way, way)]
        for way in (0, 1)
    ]
    count = len(plans[0])

    def rows_of(owner, h):
        return pl.ds(pl.multiple_of(owner * seg + h * half, half), half)

    def target(way, i):
        h, k = plans[way][i]
        return ring_chip(place + ways[way] * k, chips), h

    def across(way, i):
        to, h = target(way, i)
        return remote(
            back_ref.at[rows_of(to * 2 + 1 - core, h)], xbuf.at[way, i], xs.at[way, i], xr.at[way, i], sibling
        )

    def own_across(h):
        return remote(
            back_ref.at[rows_of(chip * 2 + 1 - core, h)], xown.at[h], os.at[h], orr.at[h], sibling
        )

    def hop(way, i):
        return remote(sbuf.at[way, i], rbuf.at[way, i], ssem.at[way, i], rsem.at[way, i], nexts[way])

    def step(way, i):
        to, h = target(way, i)
        across(way, i).wait_recv()
        total = back_ref[rows_of(to * 2 + core, h), :].astype(jnp.float32) + xbuf[way, i].astype(jnp.float32)
        if i >= 2:
            hop(way, i - 2).wait_recv()
            total = total + rbuf[way, i - 2].astype(jnp.float32)
        sbuf[way, i] = total.astype(sbuf.dtype)
        hop(way, i).start()

    for i in range(count):
        for way in (0, 1):
            across(way, i).start()
    for h in (0, 1):
        own_across(h).start()
    for i in (0, 1):
        for way in (0, 1):
            step(way, i)

    gsum[...] = jnp.zeros_like(gsum)

    @pl.loop(0, n_row)
    def _(block):
        rows = pl.ds(pl.multiple_of(block * seg, seg), seg)
        gsum[...] += lax.dot_general(
            fp_ref[rows, :], back_ref[rows, :], (((0,), (0,)), ((), ())), preferred_element_type=jnp.float32
        )

    own_rows = gw_ref.shape[0] // 2

    def half_rows(which):
        return pl.ds(pl.multiple_of(which * own_rows, own_rows), own_rows)

    gsib_out[...] = gsum[half_rows(1 - core), :].astype(gsib_out.dtype)
    sib_copy = remote(gsib_out, gsib_in, ga.at[0], ga.at[1], sibling)
    sib_copy.start()

    def spread(o):
        return remote(
            gout.at[lax.rem(chip + o, chips)], gin.at[o - 1], gb_s.at[o - 1], gb_r.at[o - 1], peers[o - 1]
        )

    def stage_b():
        sib_copy.wait_recv()
        total = gsum[half_rows(core), :] + gsib_in[...].astype(jnp.float32)
        gsum[half_rows(core), :] = total
        gout[...] = total.astype(gout.dtype).reshape(gout.shape)
        for o in range(1, chips):
            spread(o).start()

    def over_cols(o):
        return remote(gslice.at[0], gcol.at[o - 1], gc_s.at[o - 1], gc_r.at[o - 1], cols[o - 1])

    def stage_c():
        mine = pl.multiple_of(core * own_rows + chip * rows_each, rows_each)
        total = gsum[pl.ds(mine, rows_each), :]
        for o in range(1, chips):
            spread(o).wait_recv()
            total = total + gin[o - 1].astype(jnp.float32)
        gslice[0] = total
        for o in range(1, n_col):
            over_cols(o).start()

    def collect(o):
        return remote(gslice.at[1], gfin.at[core, chip], gd_s.at[o - 1], gd_r.at[o - 1], peers[o - 1])

    def stage_d():
        total = gslice[0]
        for o in range(1, n_col):
            over_cols(o).wait_recv()
        ordered = None
        for c in range(n_col):
            term = total
            for o in range(1, n_col):
                term = jnp.where(lax.rem(mycol - o + n_col, n_col) == c, gcol[o - 1], term)
            ordered = term if ordered is None else ordered + term
        gslice[1] = ordered
        gfin[core, chip] = ordered
        for o in range(1, chips):
            collect(o).start()

    last_copy = remote(gfin.at[core], gfin.at[core], ge.at[0], ge.at[1], sibling)

    def stage_e():
        for o in range(1, chips):
            collect(o).wait_recv()
        last_copy.start()

    stages = {2: stage_b, 4: stage_c, 5: stage_d}
    for i in range(2, count):
        for way in (0, 1):
            step(way, i)
        if i in stages:
            stages[i]()
    for h in (0, 1):
        own_across(h).wait_recv()
    stage_e()
    order = [count - 2, count - 1]
    for h in (1, 0):
        total = back_ref[rows_of(me, h), :].astype(jnp.float32) + xown[h].astype(jnp.float32)
        for way in (0, 1):
            for i in order:
                if plans[way][i][0] == h:
                    hop(way, i).wait_recv()
                    total = total + rbuf[way, i].astype(jnp.float32)
        gf_ref[pl.ds(h * half, half), :] = lax.dot_general(
            total.astype(jnp.bfloat16), w_ref[...], (((1,), (1,)), ((), ())), preferred_element_type=jnp.float32
        ).astype(gf_ref.dtype)
    last_copy.wait_recv()
    gw_ref[...] = gfin[...].reshape(gw_ref.shape)
    for way in (0, 1):
        for i in range(count):
            hop(way, i).wait_send()
            across(way, i).wait_send()
    for h in (0, 1):
        own_across(h).wait_send()
    sib_copy.wait_send()
    for o in range(1, chips):
        spread(o).wait_send()
        collect(o).wait_send()
    for o in range(1, n_col):
        over_cols(o).wait_send()
    last_copy.wait_send()


def scatter_sum(back_terms, feature_panel, weight, n_row, n_col):
    rows, feat_width = back_terms.shape
    seg = rows // n_row
    half = seg // 2
    chips = n_row // 2
    count = chips - 1
    in_width, out_width = weight.shape
    each = in_width // 2 // chips
    dma = pltpu.SemaphoreType.DMA
    bf16, f32 = jnp.bfloat16, jnp.float32
    return pl.pallas_call(
        functools.partial(scatter_kernel, n_row, n_col),
        out_shape=(
            jax.ShapeDtypeStruct((seg, in_width), bf16),
            jax.ShapeDtypeStruct((in_width, out_width), f32),
        ),
        in_specs=[VMEM_SPEC] * 3,
        out_specs=(VMEM_SPEC, VMEM_SPEC),
        scratch_shapes=[
            pltpu.VMEM((2, count, half, feat_width), bf16),
            pltpu.VMEM((2, half, feat_width), bf16),
            pltpu.VMEM((2, count, half, feat_width), bf16),
            pltpu.VMEM((2, count, half, feat_width), bf16),
            pltpu.VMEM((in_width, out_width), f32),
            pltpu.VMEM((in_width // 2, out_width), bf16),
            pltpu.VMEM((in_width // 2, out_width), bf16),
            pltpu.VMEM((chips, each, out_width), bf16),
            pltpu.VMEM((chips - 1, each, out_width), bf16),
            pltpu.VMEM((n_col - 1, each, out_width), f32),
            pltpu.VMEM((2, each, out_width), f32),
            pltpu.VMEM((2, chips, each, out_width), f32),
            dma((2, count)),
            dma((2, count)),
            dma((2, count)),
            dma((2, count)),
            dma((2,)),
            dma((2,)),
            dma((2,)),
            dma((chips - 1,)),
            dma((chips - 1,)),
            dma((n_col - 1,)),
            dma((n_col - 1,)),
            dma((chips - 1,)),
            dma((chips - 1,)),
            dma((2,)),
        ],
        compiler_params=pltpu.CompilerParams(
            collective_id=2, has_side_effects=True, vmem_limit_bytes=grant(10 * back_terms.size)
        ),
        name="scatter",
    )(back_terms, feature_panel, weight)


def spread_kernel(transpose, plan_ref, tiles_ref, panel_ref, out_ref, acc):
    tile_size = tiles_ref.shape[1]
    out_tiles = out_ref.shape[0] // tile_size
    pairs = plan_ref[0, plan_ref.shape[1] - 1]
    acc[...] = jnp.zeros_like(acc)
    contract = (((0,), (0,)), ((), ())) if transpose else (((1,), (0,)), ((), ()))

    def read_rows(entry):
        return panel_ref[pl.ds(pl.multiple_of(plan_ref[1, entry] * tile_size, tile_size), tile_size), :]

    def product(pair):
        entries = (2 * pair, 2 * pair + 1)
        left = jnp.concatenate([tiles_ref[plan_ref[0, e]] for e in entries], axis=0 if transpose else 1)
        right = jnp.concatenate([read_rows(e) for e in entries], axis=0)
        return lax.dot_general(left, right, contract, preferred_element_type=jnp.float32)

    def add(pair, value):
        dst = pl.multiple_of(plan_ref[2, 2 * pair] * tile_size, tile_size)
        acc[pl.ds(dst, tile_size), :] += value

    def group_step(group, carry):
        first = group * GROUP
        values = [product(first + k) for k in range(GROUP)]
        for k in range(GROUP):
            add(first + k, values[k])
        return carry

    lax.fori_loop(0, (pairs + GROUP - 1) // GROUP, group_step, 0)

    def finish(tile, carry):
        part = pl.ds(pl.multiple_of(tile * tile_size, tile_size), tile_size)
        out_ref[part, :] = acc[part, :].astype(out_ref.dtype)
        return carry

    lax.fori_loop(0, out_tiles, finish, 0)


def spread_tiles(tiles, plan, panel, out_rows, transpose):
    feat_width = panel.shape[-1]
    return pl.pallas_call(
        functools.partial(spread_kernel, transpose),
        out_shape=jax.ShapeDtypeStruct((out_rows, feat_width), jnp.bfloat16),
        in_specs=[pl.BlockSpec(memory_space=pltpu.SMEM), VMEM_SPEC, VMEM_SPEC],
        out_specs=VMEM_SPEC,
        scratch_shapes=[pltpu.VMEM((out_rows, feat_width), jnp.float32)],
        compiler_params=pltpu.CompilerParams(
            vmem_limit_bytes=grant(2 * tiles.size + 2 * panel.size + 6 * out_rows * feat_width)
        ),
        name="back" if transpose else "forth",
    )(plan, tiles, panel)


def finish_kernel(a_ref, b_ref, a_out, b_out, sems):
    copies = [
        pltpu.make_async_copy(a_ref, a_out, sems.at[0]),
        pltpu.make_async_copy(b_ref, b_out, sems.at[1]),
    ]
    for copy in copies:
        copy.start()
    for copy in copies:
        copy.wait()


def finish(a, b):
    hbm = pl.BlockSpec(memory_space=pltpu.MemorySpace.HBM)
    return pl.pallas_call(
        finish_kernel,
        out_shape=(jax.ShapeDtypeStruct(a.shape, a.dtype), jax.ShapeDtypeStruct(b.shape, b.dtype)),
        in_specs=[VMEM_SPEC] * 2,
        out_specs=(hbm, hbm),
        scratch_shapes=[pltpu.SemaphoreType.DMA((2,))],
        compiler_params=pltpu.CompilerParams(vmem_limit_bytes=grant(2 * a.size + 4 * b.size)),
        name="finish",
    )(a, b)


def body(features, grad_out, weight, tiles, tile_row, tile_col, tile_count):
    segment = features.shape[0]
    n_row, n_col = lax.axis_size("row"), lax.axis_size("col")
    feature_panel, panel, held, forth_plan, back_plan = gather_mixed(
        features, weight, tiles, tile_row, tile_col, tile_count, n_row
    )
    partial_value = spread_tiles(held, forth_plan, panel, segment * n_col, False)
    grad_block = exchange(partial_value, grad_out, n_col)
    back_terms = spread_tiles(held, back_plan, grad_block, segment * n_row, True)
    return finish(*scatter_sum(back_terms, feature_panel, weight, n_row, n_col))


def solution(mesh):
    in_specs = (
        P(("row", "col"), None),
        P(("row", "col"), None),
        P(),
        P(("row", "col"), None, None),
        P(("row", "col")),
        P(("row", "col")),
        P(("row", "col")),
    )
    out_specs = (P(("row", "col"), None), P())
    return jax.shard_map(body, mesh=mesh, in_specs=in_specs, out_specs=out_specs, check_vma=False)
```

```python
import functools

import jax
import jax.numpy as jnp
from jax import lax
from jax.experimental import pallas as pl
from jax.experimental.pallas import tpu as pltpu
from jax.sharding import PartitionSpec as P

GROUP = 8


MESH = pl.DeviceIdType.MESH
VMEM_SPEC = pl.BlockSpec(memory_space=pltpu.VMEM)


def grant(bytes_held):
    return bytes_held + 6 * 1024 * 1024


def silu_grad(preact, upstream):
    sigmoid_z = jax.nn.sigmoid(preact)
    return (upstream.astype(jnp.float32) * sigmoid_z * (1.0 + preact * (1.0 - sigmoid_z))).astype(
        jnp.bfloat16
    )


def ring_place(chip, chips):
    half = lax.div(chip, 2)
    return jnp.where(lax.rem(chip, 2) == 0, half, chips - 1 - half)


def ring_chip(place, chips):
    place = lax.rem(place + 2 * chips, chips)
    return jnp.where(place < chips // 2, 2 * place, 2 * (chips - 1 - place) + 1)


def row_device(chip, core):
    return {"row": chip * 2 + core}


def greet(partners):
    barrier = pltpu.get_barrier_semaphore()
    for partner in partners:
        pl.semaphore_signal(barrier, inc=1, device_id=partner, device_id_type=MESH)
    pl.semaphore_wait(barrier, len(partners))


def remote(src, dst, send_sem, recv_sem, device):
    return pltpu.make_async_remote_copy(
        src_ref=src, dst_ref=dst, send_sem=send_sem, recv_sem=recv_sem, device_id=device, device_id_type=MESH
    )


def pair_plan(read_row, write_row, count, width):
    f32 = jnp.float32
    slots = read_row.shape[1]
    lane = lax.broadcasted_iota(jnp.int32, (slots, slots), 1)
    sub = lax.broadcasted_iota(jnp.int32, (slots, slots), 0)

    def as_column(row):
        return jnp.sum(jnp.where(lane == sub, row, 0.0), axis=1, keepdims=True)

    read_col = as_column(jnp.broadcast_to(read_row.astype(f32), (slots, slots)))
    row = jnp.broadcast_to(write_row.astype(f32), (slots, slots))
    write_col = as_column(row)
    col = jnp.broadcast_to(write_col, (slots, slots))
    live = jnp.where((lane < count) & (sub < count), 1.0, 0.0)
    same = jnp.where(row == col, live, 0.0)
    rank_col = jnp.sum(jnp.where(lane < sub, same, 0.0), axis=1, keepdims=True)
    rank_row = jnp.sum(jnp.where(sub < lane, same, 0.0), axis=0, keepdims=True)
    odd_row = rank_row - 2.0 * jnp.floor(rank_row * 0.5)
    opens = jnp.where(lane < count, 1.0 - jnp.broadcast_to(odd_row, (slots, slots)), 0.0)
    base = jnp.sum(jnp.where(row < col, opens, 0.0), axis=1, keepdims=True)
    pairs = jnp.sum(opens, axis=1, keepdims=True)[0:1, :]
    place = lax.broadcasted_iota(jnp.int32, (slots, width), 1).astype(f32)
    slot = lax.broadcasted_iota(jnp.int32, (slots, width), 0)
    hit = jnp.where(slot < count, jnp.where(place == 2.0 * base + rank_col, 1.0, 0.0), 0.0)
    slot_at = jnp.sum(hit * (slot - slots).astype(f32), axis=0, keepdims=True) + float(slots)
    last = lax.broadcasted_iota(jnp.int32, (1, width), 1) == width - 1
    slot_at = jnp.where(last, jnp.broadcast_to(pairs, (1, width)), slot_at)
    read_at = jnp.sum(hit * read_col, axis=0, keepdims=True)
    write_at = jnp.sum(hit * write_col, axis=0, keepdims=True)
    return [part.astype(jnp.int32) for part in (slot_at, read_at, write_at)]


def gather_kernel(
    n_row, count_ref, f_hbm, w_hbm, tr_hbm, tc_hbm, tiles_hbm,
    fp_ref, mp_ref, tiles_ref, forth_ref, back_ref,
    f_ref, w_ref, tr_ref, tc_ref, ssem, rsem, xs, xr, os, orr, tsem, isem,
):
    inputs = [
        pltpu.make_async_copy(src, dst, isem.at[at])
        for at, (src, dst) in enumerate(
            ((f_hbm, f_ref), (w_hbm, w_ref), (tr_hbm, tr_ref), (tc_hbm, tc_ref))
        )
    ]
    for copy in inputs:
        copy.start()
    slots = tiles_hbm.shape[0]
    load = pltpu.make_async_copy(tiles_hbm, tiles_ref.at[pl.ds(0, slots)], tsem)
    load.start()
    chips = n_row // 2
    seg = f_ref.shape[0]
    half = seg // 2
    me = lax.axis_index("row")
    core = lax.rem(me, 2)
    chip = lax.div(me, 2)
    place = ring_place(chip, chips)
    ways = (1, -1)
    nexts = [row_device(ring_chip(place + way, chips), core) for way in ways]
    sibling = row_device(chip, 1 - core)
    greet(nexts + [sibling])
    inputs[0].wait()
    far = chips // 2
    plans = [
        [(h, k) for k in range(1, far) for h in (way, 1 - way)] + [(way, far)] for way in (0, 1)
    ]
    count = len(plans[0])

    def rows_of(owner, h):
        return pl.ds(pl.multiple_of(owner * seg + h * half, half), half)

    def origin(way, k):
        return ring_chip(place - ways[way] * k, chips)

    def hop(way, i):
        h, k = plans[way][i]
        if k == 1:
            src = f_ref.at[pl.ds(h * half, half)]
            rows = rows_of(me, h)
        else:
            rows = rows_of(origin(way, k - 1) * 2 + core, h)
            src = fp_ref.at[rows]
        return remote(src, fp_ref.at[rows], ssem.at[way, i], rsem.at[way, i], nexts[way])

    def across(way, i):
        h, k = plans[way][i]
        rows = rows_of(origin(way, k) * 2 + core, h)
        return remote(fp_ref.at[rows], fp_ref.at[rows], xs.at[way, i], xr.at[way, i], sibling)

    def own_across(h):
        return remote(
            f_ref.at[pl.ds(h * half, half)], fp_ref.at[rows_of(me, h)], os.at[h], orr.at[h], sibling
        )

    def mix(owner, h):
        rows = rows_of(owner, h)
        mp_ref[rows, :] = jnp.dot(
            fp_ref[rows, :], w_ref[...], preferred_element_type=jnp.float32
        ).astype(mp_ref.dtype)

    for i in (0, 1):
        for way in (0, 1):
            hop(way, i).start()
    for h in (0, 1):
        own_across(h).start()
    for copy in inputs[1:]:
        copy.wait()
    fp_ref[pl.ds(pl.multiple_of(me * seg, seg), seg), :] = f_ref[...]
    for h in (0, 1):
        mix(me, h)
    tiles_ref[slots] = jnp.zeros_like(tiles_ref[slots])
    tr, tc, live = tr_ref[...], tc_ref[...], count_ref[0]
    for plan_ref, reads, writes in ((forth_ref, tc, tr), (back_ref, tr, tc)):
        for line, part in enumerate(pair_plan(reads, writes, live, plan_ref.shape[1])):
            plan_ref[line : line + 1, :] = part
    for i in range(count):
        for way in (0, 1):
            hop(way, i).wait_recv()
            if i + 2 < count:
                hop(way, i + 2).start()
            across(way, i).start()
        if i == 0:
            for h in (0, 1):
                own_across(h).wait_recv()
                mix(chip * 2 + 1 - core, h)
        for way in (0, 1):
            h, k = plans[way][i]
            mix(origin(way, k) * 2 + core, h)
            if i > 0:
                h, k = plans[way][i - 1]
                across(way, i - 1).wait_recv()
                mix(origin(way, k) * 2 + 1 - core, h)
    for way in (0, 1):
        h, k = plans[way][count - 1]
        across(way, count - 1).wait_recv()
        mix(origin(way, k) * 2 + 1 - core, h)
    for way in (0, 1):
        for i in range(count):
            hop(way, i).wait_send()
            across(way, i).wait_send()
    for h in (0, 1):
        own_across(h).wait_send()
    load.wait()


def gather_mixed(features, weight, tiles, tile_row, tile_col, tile_count, n_row):
    seg, feat_width = features.shape
    count = n_row // 2 - 1
    slots, tile_size, _ = tiles.shape
    shape = jax.ShapeDtypeStruct((n_row * seg, feat_width), features.dtype)
    entries = slots + min(slots, n_row * seg // tile_size) + 2 * GROUP + 1
    plan = jax.ShapeDtypeStruct((3, -(-entries // 128) * 128), jnp.int32)
    held = jax.ShapeDtypeStruct((slots + 1, tile_size, tile_size), tiles.dtype)
    dma = pltpu.SemaphoreType.DMA
    return pl.pallas_call(
        functools.partial(gather_kernel, n_row),
        out_shape=(shape, shape, held, plan, plan),
        in_specs=[pl.BlockSpec(memory_space=pltpu.SMEM)]
        + [pl.BlockSpec(memory_space=pltpu.MemorySpace.HBM)] * 5,
        out_specs=(VMEM_SPEC,) * 5,
        scratch_shapes=[
            pltpu.VMEM(features.shape, features.dtype),
            pltpu.VMEM(weight.shape, weight.dtype),
            pltpu.VMEM((1, slots), jnp.int32),
            pltpu.VMEM((1, slots), jnp.int32),
        ]
        + [dma((2, count))] * 4
        + [dma((2,))] * 2
        + [dma, dma((4,))],
        compiler_params=pltpu.CompilerParams(
            collective_id=0,
            has_side_effects=True,
            vmem_limit_bytes=grant(4 * shape.size + 2 * held.size + 2 * features.size),
        ),
        name="gather",
    )(
        tile_count,
        *(
            pltpu.with_memory_space_constraint(array, pltpu.MemorySpace.HBM)
            for array in (
                features, weight, tile_row.reshape(1, slots), tile_col.reshape(1, slots), tiles
            )
        ),
    )


PARTS = 8


def exchange_kernel(n_col, part_ref, up_ref, out_ref, inbox, ssem, rsem, gs, gr):
    seg = up_ref.shape[0]
    step = seg // PARTS
    me = lax.axis_index("col")
    others = [lax.rem(me + o, n_col) for o in range(1, n_col)]
    greet([{"col": other} for other in others])

    def rows_of(owner, c):
        return pl.ds(pl.multiple_of(owner * seg + c * step, step), step)

    def there(o, c):
        return remote(
            part_ref.at[rows_of(others[o], c)],
            inbox.at[o, pl.ds(c * step, step)],
            ssem.at[o, c],
            rsem.at[o, c],
            {"col": others[o]},
        )

    def back(o, c):
        rows = rows_of(me, c)
        return remote(out_ref.at[rows], out_ref.at[rows], gs.at[o, c], gr.at[o, c], {"col": others[o]})

    for c in range(PARTS):
        for o in range(n_col - 1):
            there(o, c).start()
    for c in range(PARTS):
        rows = rows_of(me, c)
        total = part_ref[rows, :].astype(jnp.float32)
        for o in range(n_col - 1):
            there(o, c).wait_recv()
            total = total + inbox[o, pl.ds(c * step, step), :].astype(jnp.float32)
        out_ref[rows, :] = silu_grad(total, up_ref[pl.ds(c * step, step), :])
        for o in range(n_col - 1):
            back(o, c).start()
    for c in range(PARTS):
        for o in range(n_col - 1):
            back(o, c).wait_recv()
    for c in range(PARTS):
        for o in range(n_col - 1):
            there(o, c).wait_send()
            back(o, c).wait_send()


def exchange(partial_value, grad_out, n_col):
    seg, feat_width = grad_out.shape
    dma = pltpu.SemaphoreType.DMA
    return pl.pallas_call(
        functools.partial(exchange_kernel, n_col),
        out_shape=jax.ShapeDtypeStruct(partial_value.shape, jnp.bfloat16),
        in_specs=[VMEM_SPEC] * 2,
        out_specs=VMEM_SPEC,
        scratch_shapes=[pltpu.VMEM((n_col - 1, seg, feat_width), jnp.bfloat16)]
        + [dma((n_col - 1, PARTS))] * 4,
        compiler_params=pltpu.CompilerParams(
            collective_id=1, has_side_effects=True, vmem_limit_bytes=grant(6 * partial_value.size)
        ),
        name="exchange",
    )(partial_value, grad_out)


def scatter_kernel(
    n_row, n_col, back_ref, fp_ref, w_ref, gf_ref, gw_ref, xbuf, xown, sbuf, rbuf,
    gsum, gsib_out, gsib_in, gout, gin, gcol, gslice, gfin,
    ssem, rsem, xs, xr, os, orr, ga, gb_s, gb_r, gc_s, gc_r, gd_s, gd_r, ge,
):
    chips = n_row // 2
    seg = gf_ref.shape[0]
    half = seg // 2
    me = lax.axis_index("row")
    mycol = lax.axis_index("col")
    core = lax.rem(me, 2)
    chip = lax.div(me, 2)
    place = ring_place(chip, chips)
    ways = (1, -1)
    nexts = [row_device(ring_chip(place + way, chips), core) for way in ways]
    sibling = row_device(chip, 1 - core)
    peers = [row_device(lax.rem(chip + o, chips), core) for o in range(1, chips)]
    cols = [{"col": lax.rem(mycol + o, n_col)} for o in range(1, n_col)]
    width = gw_ref.shape[1]
    rows_each = gw_ref.shape[0] // 2 // chips
    greet(peers + [sibling] + cols)
    far = chips // 2
    plans = [
        [(way, far)] + [(h, k) for k in range(far - 1, 0, -1) for h in (1 - way, way)]
        for way in (0, 1)
    ]
    count = len(plans[0])

    def rows_of(owner, h):
        return pl.ds(pl.multiple_of(owner * seg + h * half, half), half)

    def target(way, i):
        h, k = plans[way][i]
        return ring_chip(place + ways[way] * k, chips), h

    def across(way, i):
        to, h = target(way, i)
        return remote(
            back_ref.at[rows_of(to * 2 + 1 - core, h)], xbuf.at[way, i], xs.at[way, i], xr.at[way, i], sibling
        )

    def own_across(h):
        return remote(
            back_ref.at[rows_of(chip * 2 + 1 - core, h)], xown.at[h], os.at[h], orr.at[h], sibling
        )

    def hop(way, i):
        return remote(sbuf.at[way, i], rbuf.at[way, i], ssem.at[way, i], rsem.at[way, i], nexts[way])

    def step(way, i):
        to, h = target(way, i)
        across(way, i).wait_recv()
        total = back_ref[rows_of(to * 2 + core, h), :].astype(jnp.float32) + xbuf[way, i].astype(jnp.float32)
        if i >= 2:
            hop(way, i - 2).wait_recv()
            total = total + rbuf[way, i - 2].astype(jnp.float32)
        sbuf[way, i] = total.astype(sbuf.dtype)
        hop(way, i).start()

    for i in range(count):
        for way in (0, 1):
            across(way, i).start()
    for h in (0, 1):
        own_across(h).start()
    for i in (0, 1):
        for way in (0, 1):
            step(way, i)

    gsum[...] = jnp.zeros_like(gsum)

    def terms(first, past):
        @pl.loop(first, past)
        def _(block):
            rows = pl.ds(pl.multiple_of(block * seg, seg), seg)
            gsum[...] += lax.dot_general(
                fp_ref[rows, :], back_ref[rows, :], (((0,), (0,)), ((), ())), preferred_element_type=jnp.float32
            )

    terms(0, chips)
    own_rows = gw_ref.shape[0] // 2

    def half_rows(which):
        return pl.ds(pl.multiple_of(which * own_rows, own_rows), own_rows)

    sib_copy = remote(gsib_out, gsib_in, ga.at[0], ga.at[1], sibling)

    def stage_a():
        terms(chips, n_row)
        gsib_out[...] = gsum[half_rows(1 - core), :].astype(gsib_out.dtype)
        sib_copy.start()

    def spread(o):
        return remote(
            gout.at[lax.rem(chip + o, chips)], gin.at[o - 1], gb_s.at[o - 1], gb_r.at[o - 1], peers[o - 1]
        )

    def stage_b():
        sib_copy.wait_recv()
        total = gsum[half_rows(core), :] + gsib_in[...].astype(jnp.float32)
        gsum[half_rows(core), :] = total
        gout[...] = total.astype(gout.dtype).reshape(gout.shape)
        for o in range(1, chips):
            spread(o).start()

    def over_cols(o):
        return remote(gslice.at[0], gcol.at[o - 1], gc_s.at[o - 1], gc_r.at[o - 1], cols[o - 1])

    def stage_c():
        mine = pl.multiple_of(core * own_rows + chip * rows_each, rows_each)
        total = gsum[pl.ds(mine, rows_each), :]
        for o in range(1, chips):
            spread(o).wait_recv()
            total = total + gin[o - 1].astype(jnp.float32)
        gslice[0] = total
        for o in range(1, n_col):
            over_cols(o).start()

    def collect(o):
        return remote(gslice.at[1], gfin.at[core, chip], gd_s.at[o - 1], gd_r.at[o - 1], peers[o - 1])

    def stage_d():
        total = gslice[0]
        for o in range(1, n_col):
            over_cols(o).wait_recv()
        ordered = None
        for c in range(n_col):
            term = total
            for o in range(1, n_col):
                term = jnp.where(lax.rem(mycol - o + n_col, n_col) == c, gcol[o - 1], term)
            ordered = term if ordered is None else ordered + term
        gslice[1] = ordered
        gfin[core, chip] = ordered
        for o in range(1, chips):
            collect(o).start()

    last_copy = remote(gfin.at[core], gfin.at[core], ge.at[0], ge.at[1], sibling)

    def stage_e():
        for o in range(1, chips):
            collect(o).wait_recv()
        last_copy.start()

    stages = {2: stage_a, 3: stage_b, 4: stage_c, 5: stage_d}
    for i in range(2, count):
        for way in (0, 1):
            step(way, i)
        if i in stages:
            stages[i]()
    for h in (0, 1):
        own_across(h).wait_recv()
    stage_e()
    order = [count - 2, count - 1]
    for h in (1, 0):
        total = back_ref[rows_of(me, h), :].astype(jnp.float32) + xown[h].astype(jnp.float32)
        for way in (0, 1):
            for i in order:
                if plans[way][i][0] == h:
                    hop(way, i).wait_recv()
                    total = total + rbuf[way, i].astype(jnp.float32)
        gf_ref[pl.ds(h * half, half), :] = lax.dot_general(
            total.astype(jnp.bfloat16), w_ref[...], (((1,), (1,)), ((), ())), preferred_element_type=jnp.float32
        ).astype(gf_ref.dtype)
    last_copy.wait_recv()
    gw_ref[...] = gfin[...].reshape(gw_ref.shape)
    for way in (0, 1):
        for i in range(count):
            hop(way, i).wait_send()
            across(way, i).wait_send()
    for h in (0, 1):
        own_across(h).wait_send()
    sib_copy.wait_send()
    for o in range(1, chips):
        spread(o).wait_send()
        collect(o).wait_send()
    for o in range(1, n_col):
        over_cols(o).wait_send()
    last_copy.wait_send()


def scatter_sum(back_terms, feature_panel, weight, n_row, n_col):
    rows, feat_width = back_terms.shape
    seg = rows // n_row
    half = seg // 2
    chips = n_row // 2
    count = chips - 1
    in_width, out_width = weight.shape
    each = in_width // 2 // chips
    dma = pltpu.SemaphoreType.DMA
    bf16, f32 = jnp.bfloat16, jnp.float32
    return pl.pallas_call(
        functools.partial(scatter_kernel, n_row, n_col),
        out_shape=(
            jax.ShapeDtypeStruct((seg, in_width), bf16),
            jax.ShapeDtypeStruct((in_width, out_width), f32),
        ),
        in_specs=[VMEM_SPEC] * 3,
        out_specs=(VMEM_SPEC, VMEM_SPEC),
        scratch_shapes=[
            pltpu.VMEM((2, count, half, feat_width), bf16),
            pltpu.VMEM((2, half, feat_width), bf16),
            pltpu.VMEM((2, count, half, feat_width), bf16),
            pltpu.VMEM((2, count, half, feat_width), bf16),
            pltpu.VMEM((in_width, out_width), f32),
            pltpu.VMEM((in_width // 2, out_width), bf16),
            pltpu.VMEM((in_width // 2, out_width), bf16),
            pltpu.VMEM((chips, each, out_width), bf16),
            pltpu.VMEM((chips - 1, each, out_width), bf16),
            pltpu.VMEM((n_col - 1, each, out_width), f32),
            pltpu.VMEM((2, each, out_width), f32),
            pltpu.VMEM((2, chips, each, out_width), f32),
            dma((2, count)),
            dma((2, count)),
            dma((2, count)),
            dma((2, count)),
            dma((2,)),
            dma((2,)),
            dma((2,)),
            dma((chips - 1,)),
            dma((chips - 1,)),
            dma((n_col - 1,)),
            dma((n_col - 1,)),
            dma((chips - 1,)),
            dma((chips - 1,)),
            dma((2,)),
        ],
        compiler_params=pltpu.CompilerParams(
            collective_id=2, has_side_effects=True, vmem_limit_bytes=grant(10 * back_terms.size)
        ),
        name="scatter",
    )(back_terms, feature_panel, weight)


def spread_kernel(transpose, plan_ref, tiles_ref, panel_ref, out_ref, acc):
    tile_size = tiles_ref.shape[1]
    out_tiles = out_ref.shape[0] // tile_size
    pairs = plan_ref[0, plan_ref.shape[1] - 1]
    acc[...] = jnp.zeros_like(acc)
    contract = (((0,), (0,)), ((), ())) if transpose else (((1,), (0,)), ((), ()))

    def read_rows(entry):
        return panel_ref[pl.ds(pl.multiple_of(plan_ref[1, entry] * tile_size, tile_size), tile_size), :]

    def product(pair):
        entries = (2 * pair, 2 * pair + 1)
        left = jnp.concatenate([tiles_ref[plan_ref[0, e]] for e in entries], axis=0 if transpose else 1)
        right = jnp.concatenate([read_rows(e) for e in entries], axis=0)
        return lax.dot_general(left, right, contract, preferred_element_type=jnp.float32)

    def add(pair, value):
        dst = pl.multiple_of(plan_ref[2, 2 * pair] * tile_size, tile_size)
        acc[pl.ds(dst, tile_size), :] += value

    def group_step(group, carry):
        first = group * GROUP
        values = [product(first + k) for k in range(GROUP)]
        for k in range(GROUP):
            add(first + k, values[k])
        return carry

    lax.fori_loop(0, (pairs + GROUP - 1) // GROUP, group_step, 0)

    def finish(tile, carry):
        part = pl.ds(pl.multiple_of(tile * tile_size, tile_size), tile_size)
        out_ref[part, :] = acc[part, :].astype(out_ref.dtype)
        return carry

    lax.fori_loop(0, out_tiles, finish, 0)


def spread_tiles(tiles, plan, panel, out_rows, transpose):
    feat_width = panel.shape[-1]
    return pl.pallas_call(
        functools.partial(spread_kernel, transpose),
        out_shape=jax.ShapeDtypeStruct((out_rows, feat_width), jnp.bfloat16),
        in_specs=[pl.BlockSpec(memory_space=pltpu.SMEM), VMEM_SPEC, VMEM_SPEC],
        out_specs=VMEM_SPEC,
        scratch_shapes=[pltpu.VMEM((out_rows, feat_width), jnp.float32)],
        compiler_params=pltpu.CompilerParams(
            vmem_limit_bytes=grant(2 * tiles.size + 2 * panel.size + 6 * out_rows * feat_width)
        ),
        name="back" if transpose else "forth",
    )(plan, tiles, panel)


def finish_kernel(a_ref, b_ref, a_out, b_out, sems):
    copies = [
        pltpu.make_async_copy(a_ref, a_out, sems.at[0]),
        pltpu.make_async_copy(b_ref, b_out, sems.at[1]),
    ]
    for copy in copies:
        copy.start()
    for copy in copies:
        copy.wait()


def finish(a, b):
    hbm = pl.BlockSpec(memory_space=pltpu.MemorySpace.HBM)
    return pl.pallas_call(
        finish_kernel,
        out_shape=(jax.ShapeDtypeStruct(a.shape, a.dtype), jax.ShapeDtypeStruct(b.shape, b.dtype)),
        in_specs=[VMEM_SPEC] * 2,
        out_specs=(hbm, hbm),
        scratch_shapes=[pltpu.SemaphoreType.DMA((2,))],
        compiler_params=pltpu.CompilerParams(vmem_limit_bytes=grant(2 * a.size + 4 * b.size)),
        name="finish",
    )(a, b)


def body(features, grad_out, weight, tiles, tile_row, tile_col, tile_count):
    segment = features.shape[0]
    n_row, n_col = lax.axis_size("row"), lax.axis_size("col")
    feature_panel, panel, held, forth_plan, back_plan = gather_mixed(
        features, weight, tiles, tile_row, tile_col, tile_count, n_row
    )
    partial_value = spread_tiles(held, forth_plan, panel, segment * n_col, False)
    grad_block = exchange(partial_value, grad_out, n_col)
    back_terms = spread_tiles(held, back_plan, grad_block, segment * n_row, True)
    return finish(*scatter_sum(back_terms, feature_panel, weight, n_row, n_col))


def solution(mesh):
    in_specs = (
        P(("row", "col"), None),
        P(("row", "col"), None),
        P(),
        P(("row", "col"), None, None),
        P(("row", "col")),
        P(("row", "col")),
        P(("row", "col")),
    )
    out_specs = (P(("row", "col"), None), P())
    return jax.shard_map(body, mesh=mesh, in_specs=in_specs, out_specs=out_specs, check_vma=False)
```
